32 devices in a mesh: groups: 2 (over y), seq: 16 (over z, x, core).
Axes of the slice: x: 2, y: 2, z: 4, core: 2. Of those that a mesh axis runs over, the one named last changes fastest.
Arguments:
- frames: bfloat16 [64, 32, 128, 128], P(('groups', 'seq')), parts along dimension 0, may hold values from -6 to 6
- w_spatial: bfloat16 [3, 3, 128, 128], replicated, may hold values from -0.1875 to 0.1875
- w_temporal: bfloat16 [2, 3, 128, 128], replicated, may hold values from -0.3125 to 0.3125
- dilations: int32 [2], replicated, may hold values from 1 to 16
- offsets: int32 [2, 3], replicated, may hold values from 0 to 3
- cotangent: bfloat16 [64, 1024, 128], P('groups', 'seq'), parts along dimension 0, may hold values from -0.011962891 to 0.011962891
Outputs:
- features: bfloat16 [64, 1024, 128], P('groups', 'seq'), parts along dimension 0
- grad_spatial: float32 [6, 3, 128, 128], P('groups'), parts along dimension 0
- grad_temporal: float32 [4, 3, 128, 128], P('groups'), parts along dimension 0
The draws below stay inside these ranges and needn't reach their ends.
There are 2 independent parts, one for each index of `groups`. The reference program is written for one: setup_inputs(seed, part) draws one part's arguments, and reference() takes and returns one part's arrays. A program takes and returns all parts, laid end to end along the dimension named above; an argument that names none is the same for every part. Nothing has to cross between parts.
All inputs are finite; a program needn't handle non-finite values.
Results may differ from the reference program's by a relative error of at most 0.0067.
Values may be sent and summed in bfloat16 or wider, within the bound.
No kernel may reach another device: no remote copies, remote signals or barrier semaphores. Data moves between devices by JAX's collectives and lax.ppermute only.
A program may use at most 64 MiB of HBM per device.

```python
import jax
import jax.numpy as jnp
from jax import lax

C = 128
W_IN = 128
H_IN = 32
LAYERS = 2
KT = 3
PIX = 1024
FRAMES = 32
N_SEQ = 16


def draw_dilations(key, part):
    first, second = jax.random.split(jax.random.fold_in(key, 11))
    values = jax.random.randint(first, (LAYERS,), 1, 17)
    where_top = jax.random.randint(second, (), 0, LAYERS)
    return jnp.where(jnp.arange(LAYERS) == where_top, 16, values).astype(jnp.int32)


def draw_offsets(key, part):
    first, second = jax.random.split(jax.random.fold_in(key, 23))
    values = jax.random.randint(first, (LAYERS * KT,), 0, 4)
    where_top = jax.random.randint(second, (), 0, LAYERS * KT)
    values = jnp.where(jnp.arange(LAYERS * KT) == where_top, 3, values)
    return values.reshape(LAYERS, KT).astype(jnp.int32)


def block_scale(own_key, dims, pieces, least, top_value):
    level = 1.0
    for axis_at, shards_of in pieces:
        steps = jax.random.uniform(jax.random.fold_in(jax.random.fold_in(own_key, 6), axis_at), (shards_of,), jnp.float32, least / len(pieces), top_value / len(pieces))
        level = level * jnp.repeat(jnp.exp(steps), dims[axis_at] // shards_of).reshape((-1,) + (1,) * (len(dims) - 1 - axis_at))
    return level


def gaussian(own_key, dims, deviation, most, cuts=(), kind=jnp.bfloat16):
    loudness = block_scale(own_key, dims, cuts, -0.22, 0.18) if cuts else 1.0
    result = jax.random.normal(own_key, dims, jnp.float32) * deviation * loudness
    return jnp.minimum(jnp.maximum(result, -most), most).astype(kind)


def setup_inputs(seed: int = 0, part: int = 0) -> dict:
    keys = jax.random.split(jax.random.key(seed), 7)
    own_keys = jax.random.split(jax.random.fold_in(keys[6], part), 7)
    frames = gaussian(own_keys[0], (FRAMES, H_IN, W_IN, C), 1.0, 6.0, ((0, 16),))
    w_spatial = gaussian(keys[1], (3, 3, C, C), (9 * C) ** -0.5, 0.1875)
    w_temporal = gaussian(keys[2], (LAYERS, KT, C, C), (KT * C) ** -0.5, 0.3125)
    dilations = draw_dilations(jax.random.fold_in(keys[6], 71), part)
    offsets = draw_offsets(jax.random.fold_in(keys[6], 71), part)
    cotangent = gaussian(own_keys[5], (FRAMES, PIX, C), 0.002, 0.011962891, ((1, 16),))
    return {"frames": frames, "w_spatial": w_spatial, "w_temporal": w_temporal, "dilations": dilations, "offsets": offsets, "cotangent": cotangent}


def padded_view(frame):
    height, width, channels = frame.shape
    padded = jnp.pad(frame, ((1, 1), (1, 1), (0, 0)))
    return padded.reshape(height // 2 + 1, 2, width // 2 + 1, 2, channels)

def window(view, row_tap, col_tap):
    out_rows = view.shape[0] - 1
    out_cols = view.shape[2] - 1
    return view[row_tap // 2:row_tap // 2 + out_rows, row_tap % 2, col_tap // 2:col_tap // 2 + out_cols, col_tap % 2, :]

def spatial_frame(frame, w_spatial):
    view = padded_view(frame)
    channels = frame.shape[2]
    total = jnp.zeros((view.shape[0] - 1) * (view.shape[2] - 1) * 0 + (view.shape[0] - 1) * (view.shape[2] - 1), jnp.float32)
    total = jnp.zeros(((view.shape[0] - 1) * (view.shape[2] - 1), channels), jnp.float32)
    for row_tap in range(3):
        for col_tap in range(3):
            patch = window(view, row_tap, col_tap).reshape(-1, channels)
            total = total + jnp.dot(patch, w_spatial[row_tap, col_tap], preferred_element_type=jnp.float32)
    return total.astype(jnp.bfloat16)

def spatial_frame_grad(frame, back):
    view = padded_view(frame)
    channels = frame.shape[2]
    rows = []
    for row_tap in range(3):
        cols = []
        for col_tap in range(3):
            patch = window(view, row_tap, col_tap).reshape(-1, channels)
            cols.append(lax.dot_general(patch, back, (((0,), (0,)), ((), ())), preferred_element_type=jnp.float32))
        rows.append(jnp.stack(cols))
    return jnp.stack(rows)

def delayed(values, delay):
    length = values.shape[0]
    delay = jnp.minimum(delay, length).astype(jnp.int32)
    joined = jnp.concatenate([jnp.zeros_like(values), values], 0)
    return lax.dynamic_slice_in_dim(joined, (length - delay).astype(jnp.int32), length, 0)

def advanced(values, delay):
    length = values.shape[0]
    delay = jnp.minimum(delay, length).astype(jnp.int32)
    joined = jnp.concatenate([values, jnp.zeros_like(values)], 0)
    return lax.dynamic_slice_in_dim(joined, delay, length, 0)

def temporal_block(start, cot_block, w_temporal, delays):
    length, pixels, channels = start.shape
    layer_count, tap_count = (w_temporal.shape[0], w_temporal.shape[1])
    states = [start]
    activations = []
    for layer in range(layer_count):
        state = states[-1]
        total = jnp.zeros((length * pixels, channels), jnp.float32)
        for tap in range(tap_count):
            moved = delayed(state, delays[layer, tap]).reshape(-1, channels)
            total = total + jnp.dot(moved, w_temporal[layer, tap], preferred_element_type=jnp.float32)
        activ = jnp.tanh(total).reshape(length, pixels, channels)
        activations.append(activ)
        states.append((state.astype(jnp.float32) + activ).astype(jnp.bfloat16))
    grad_state = cot_block.astype(jnp.float32)
    grads = [None] * layer_count
    for layer in reversed(range(layer_count)):
        activ = activations[layer]
        dz_flat = (grad_state * (1.0 - activ * activ)).astype(jnp.bfloat16).reshape(-1, channels)
        layer_grads = []
        for tap in range(tap_count):
            moved = delayed(states[layer], delays[layer, tap]).reshape(-1, channels)
            layer_grads.append(lax.dot_general(moved, dz_flat, (((0,), (0,)), ((), ())), preferred_element_type=jnp.float32))
            backward = jnp.dot(dz_flat, w_temporal[layer, tap].T, preferred_element_type=jnp.float32)
            grad_state = grad_state + advanced(backward.reshape(length, pixels, channels), delays[layer, tap])
        grads[layer] = jnp.stack(layer_grads)
    return (states[-1], grad_state.astype(jnp.bfloat16), jnp.stack(grads))

def reference(frames, w_spatial, w_temporal, dilations, offsets, cotangent):
    delays = (offsets * dilations[:, None]).astype(jnp.int32)
    spatial = lax.map(lambda frame: spatial_frame(frame, w_spatial), frames)
    pixels_dev = PIX // N_SEQ
    blocked = spatial.reshape(FRAMES, N_SEQ, pixels_dev, C).transpose(1, 0, 2, 3)
    cot_blocks = cotangent.reshape(FRAMES, N_SEQ, pixels_dev, C).transpose(1, 0, 2, 3)

    def block_step(carry, pair):
        final, back, grads = temporal_block(pair[0], pair[1], w_temporal, delays)
        return (carry + grads, (final, back))
    grad_temporal, outputs = lax.scan(block_step, jnp.zeros((LAYERS, KT, C, C), jnp.float32), (blocked, cot_blocks))
    features = outputs[0].transpose(1, 0, 2, 3).reshape(FRAMES, PIX, C)
    back_maps = outputs[1].transpose(1, 0, 2, 3).reshape(FRAMES, PIX, C)

    def frame_step(carry, pair):
        return (carry + spatial_frame_grad(pair[0], pair[1]), None)
    grad_spatial, unused = lax.scan(frame_step, jnp.zeros((3, 3, C, C), jnp.float32), (frames, back_maps))
    return (features, grad_spatial, grad_temporal)
```

```python
import functools

import jax
import jax.numpy as jnp
from jax import lax
from jax.experimental import pallas as pl
from jax.experimental.pallas import tpu as pltpu
from jax.sharding import PartitionSpec as P

VMEM_LIMIT = 56 * 1024 * 1024


def conv_kernel(x_ref, w_ref, out_ref, planes_ref):
    height, width, channels = x_ref.shape[1:]
    out_rows, out_cols = height // 2, width // 2
    chunks, chunk_pixels = out_ref.shape[0], out_ref.shape[2]
    tap = lax.broadcasted_iota(jnp.int32, (3 * out_cols, width), 0)
    col = lax.broadcasted_iota(jnp.int32, (3 * out_cols, width), 1)
    wanted = 2 * lax.rem(tap, out_cols) + lax.div(tap, out_cols) - 1
    pick = jnp.where(col == wanted, 1.0, 0.0).astype(jnp.bfloat16)
    zero = jnp.zeros((out_cols, channels), jnp.bfloat16)
    for col_tap in range(3):
        planes_ref[col_tap, 0, 0] = zero
    for row in range(height):
        picked = jnp.dot(pick, x_ref[0, row], preferred_element_type=jnp.float32)
        picked = picked.astype(jnp.bfloat16)
        for col_tap in range(3):
            planes_ref[col_tap, 0, row + 1] = picked[
                col_tap * out_cols : (col_tap + 1) * out_cols
            ]
    weights = w_ref[...].reshape(9 * channels, channels)
    step = 4
    for first in range(0, out_rows, step):
        parts = []
        for row_tap in range(3):
            for col_tap in range(3):
                parts.append(
                    jnp.concatenate(
                        [
                            planes_ref[col_tap, 0, 2 * row + row_tap]
                            for row in range(first, first + step)
                        ],
                        0,
                    )
                )
        total = jnp.dot(
            jnp.concatenate(parts, 1), weights, preferred_element_type=jnp.float32
        ).astype(jnp.bfloat16)
        count = step * out_cols // chunk_pixels
        out_ref[pl.ds(first * out_cols // chunk_pixels, count), 0] = total.reshape(
            count, chunk_pixels, channels
        )


def conv(frames, w_spatial, n):
    count, height, width, channels = frames.shape
    out_rows, out_cols = height // 2, width // 2
    pixels = out_rows * out_cols
    return pl.pallas_call(
        conv_kernel,
        grid=(count,),
        in_specs=[
            pl.BlockSpec((1, height, width, channels), lambda f: (f, 0, 0, 0)),
            pl.BlockSpec((3, 3, channels, channels), lambda f: (0, 0, 0, 0)),
        ],
        out_specs=[
            pl.BlockSpec((n, 1, pixels // n, channels), lambda f: (0, f, 0, 0)),
            pl.BlockSpec((3, 1, height + 1, out_cols, channels), lambda f: (0, f, 0, 0, 0)),
        ],
        out_shape=[
            jax.ShapeDtypeStruct((n, count, pixels // n, channels), jnp.bfloat16),
            jax.ShapeDtypeStruct((3, count, height + 1, out_cols, channels), jnp.bfloat16),
        ],
        compiler_params=pltpu.CompilerParams(vmem_limit_bytes=VMEM_LIMIT),
        name="conv",
    )(frames, w_spatial)


def temporal_kernel(
    length, dil_ref, off_ref, start_ref, cot_ref, w_ref, feat_ref, back_ref, grad_ref, state, act, dz, grad, acc
):
    layers, taps, channels = w_ref.shape[:3]
    rows = start_ref.shape[0]
    pixels = rows // length
    chunk = min(512, rows)
    starts = range(0, rows, chunk)

    def shift(layer, tap):
        delay = jnp.minimum(off_ref[layer, tap] * dil_ref[layer], length)
        return pl.multiple_of(delay * pixels, pixels)

    shifts = [[shift(layer, tap) for tap in range(taps)] for layer in range(layers)]

    def lagged(layer, at):
        return jnp.concatenate(
            [
                state[layer, pl.ds(pl.multiple_of(rows + at - s, pixels), chunk), :]
                for s in shifts[layer]
            ],
            1,
        )

    def led(at):
        return lambda layer: jnp.concatenate(
            [dz[pl.ds(pl.multiple_of(at + s, pixels), chunk), :] for s in shifts[layer]], 1
        )

    def outer(layer, first, values, moved):
        part = lax.dot_general(
            values, moved, (((0,), (0,)), ((), ())), preferred_element_type=jnp.float32
        )
        acc[layer] = part if first else acc[layer] + part

    blank = jnp.zeros((rows, channels), jnp.bfloat16)
    for layer in range(layers):
        state[layer, pl.ds(0, rows), :] = blank
    dz[pl.ds(rows, rows), :] = blank
    state[0, pl.ds(rows, rows), :] = start_ref[...]
    down = [w_ref[layer].reshape(taps * channels, channels) for layer in range(layers)]
    up = [
        jnp.concatenate([w_ref[layer, tap].T for tap in range(taps)], 0)
        for layer in range(layers)
    ]
    for layer in range(layers):
        last = layer == layers - 1
        for at in starts:
            moved = lagged(layer, at)
            activ = jnp.tanh(jnp.dot(moved, down[layer], preferred_element_type=jnp.float32))
            held = state[layer, pl.ds(rows + at, chunk), :].astype(jnp.float32)
            following = (held + activ).astype(jnp.bfloat16)
            if last:
                feat_ref[pl.ds(at, chunk), :] = following
                cot = cot_ref[pl.ds(at, chunk), :].astype(jnp.float32)
                values = (cot * (1.0 - activ * activ)).astype(jnp.bfloat16)
                dz[pl.ds(at, chunk), :] = values
                outer(layer, at == 0, values, moved)
            else:
                state[layer + 1, pl.ds(rows + at, chunk), :] = following
                act[layer, pl.ds(at, chunk), :] = activ
    for layer in reversed(range(layers)):
        for at in starts:
            here = pl.ds(at, chunk)
            if layer == layers - 1:
                before = cot_ref[here, :].astype(jnp.float32)
            else:
                before = grad[here, :]
            grad[here, :] = before + jnp.dot(
                led(at)(layer), up[layer], preferred_element_type=jnp.float32
            )
        if layer > 0:
            for at in starts:
                here = pl.ds(at, chunk)
                activ = act[layer - 1, here, :]
                values = (grad[here, :] * (1.0 - activ * activ)).astype(jnp.bfloat16)
                dz[here, :] = values
                outer(layer - 1, at == 0, values, lagged(layer - 1, at))
    back_ref[...] = grad[...].astype(jnp.bfloat16)
    for layer in range(layers):
        for tap in range(taps):
            grad_ref[layer, tap] = acc[layer, :, tap * channels : (tap + 1) * channels].T


def temporal(start, cotangent, w_temporal, dilations, offsets, length):
    rows, channels = start.shape
    layers, taps = w_temporal.shape[:2]
    vmem = pl.BlockSpec(memory_space=pltpu.VMEM)
    smem = pl.BlockSpec(memory_space=pltpu.SMEM)
    return pl.pallas_call(
        functools.partial(temporal_kernel, length),
        in_specs=[smem, smem, vmem, vmem, vmem],
        out_specs=[vmem, vmem, vmem],
        out_shape=[
            jax.ShapeDtypeStruct((rows, channels), jnp.bfloat16),
            jax.ShapeDtypeStruct((rows, channels), jnp.bfloat16),
            jax.ShapeDtypeStruct((layers, taps, channels, channels), jnp.float32),
        ],
        scratch_shapes=[
            pltpu.VMEM((layers, 2 * rows, channels), jnp.bfloat16),
            pltpu.VMEM((max(layers - 1, 1), rows, channels), jnp.float32),
            pltpu.VMEM((2 * rows, channels), jnp.bfloat16),
            pltpu.VMEM((rows, channels), jnp.float32),
            pltpu.VMEM((layers, channels, taps * channels), jnp.float32),
        ],
        compiler_params=pltpu.CompilerParams(vmem_limit_bytes=VMEM_LIMIT),
        name="temporal",
    )(dilations, offsets, start, cotangent, w_temporal)


def outer_kernel(back_ref, planes_ref, out_ref, acc):
    chunks, _, chunk_pixels, channels = back_ref.shape
    out_rows = (planes_ref.shape[2] - 1) // 2
    out_cols = planes_ref.shape[3]
    back = back_ref[:, 0].reshape(chunks * chunk_pixels, channels)
    frame = pl.program_id(0)
    for row_tap in range(3):
        parts = []
        for col_tap in range(3):
            rows = [planes_ref[col_tap, 0, 2 * row + row_tap] for row in range(out_rows)]
            parts.append(jnp.concatenate(rows, 0))
        part = lax.dot_general(
            back,
            jnp.concatenate(parts, 1),
            (((0,), (0,)), ((), ())),
            preferred_element_type=jnp.float32,
        )

        @pl.when(frame == 0)
        def _():
            acc[row_tap] = part

        @pl.when(frame > 0)
        def _():
            acc[row_tap] += part

    @pl.when(frame == pl.num_programs(0) - 1)
    def _():
        for row_tap in range(3):
            for col_tap in range(3):
                out_ref[row_tap, col_tap] = acc[
                    row_tap, :, col_tap * channels : (col_tap + 1) * channels
                ].T


def outer(back, planes):
    chunks, count, chunk_pixels, channels = back.shape
    return pl.pallas_call(
        outer_kernel,
        grid=(count,),
        in_specs=[
            pl.BlockSpec((chunks, 1, chunk_pixels, channels), lambda f: (0, f, 0, 0)),
            pl.BlockSpec((3, 1) + planes.shape[2:], lambda f: (0, f, 0, 0, 0)),
        ],
        out_specs=pl.BlockSpec((3, 3, channels, channels), lambda f: (0, 0, 0, 0)),
        out_shape=jax.ShapeDtypeStruct((3, 3, channels, channels), jnp.float32),
        scratch_shapes=[pltpu.VMEM((3, channels, 3 * channels), jnp.float32)],
        compiler_params=pltpu.CompilerParams(vmem_limit_bytes=VMEM_LIMIT),
        name="outer",
    )(back, planes)


def reduce_all(values, n):
    me = lax.axis_index("seq")

    def swap(x, bit):
        return lax.ppermute(x, "seq", [(i, i ^ (1 << bit)) for i in range(n)])

    bits = n.bit_length() - 1
    halved = min(2, bits)
    for bit in range(halved):
        half = values.shape[0] // 2
        upper = (me >> bit) & 1
        pieces = values.reshape(2, half, -1)
        mine = lax.dynamic_index_in_dim(pieces, upper, 0, keepdims=False)
        other = lax.dynamic_index_in_dim(pieces, 1 - upper, 0, keepdims=False)
        values = mine + swap(other.astype(jnp.bfloat16), bit).astype(jnp.float32)
    for bit in range(halved, bits):
        sent = values.astype(jnp.bfloat16)
        values = sent.astype(jnp.float32) + swap(sent, bit).astype(jnp.float32)
    values = values.astype(jnp.bfloat16)
    for bit in reversed(range(halved)):
        upper = (me >> bit) & 1
        got = swap(values, bit)
        values = jnp.where(
            upper == 0, jnp.concatenate([values, got], 0), jnp.concatenate([got, values], 0)
        )
    return values.astype(jnp.float32)


def local(n, frames, w_spatial, w_temporal, dilations, offsets, cotangent):
    count, height, width, channels = frames.shape
    length, pixels = cotangent.shape[:2]
    maps, planes = conv(frames, w_spatial, n)
    start = lax.all_to_all(
        maps.reshape(n, count * pixels, channels), "seq", split_axis=0, concat_axis=0, tiled=True
    )
    features, grad_maps, grad_temporal = temporal(
        start.reshape(length * pixels, channels),
        cotangent.reshape(length * pixels, channels),
        w_temporal,
        dilations,
        offsets,
        length,
    )
    back = lax.all_to_all(
        grad_maps.reshape(n, count * pixels, channels), "seq", split_axis=0, concat_axis=0, tiled=True
    )
    grad_spatial = outer(back.reshape(n, count, pixels, channels), planes)
    both = jnp.concatenate(
        [grad_spatial.reshape(-1, channels), grad_temporal.reshape(-1, channels)], 0
    )
    both = reduce_all(both, n)
    cut = grad_spatial.size // channels
    return (
        features.reshape(length, pixels, channels),
        both[:cut].reshape(grad_spatial.shape),
        both[cut:].reshape(grad_temporal.shape),
    )


def solution(mesh):
    in_specs = (
        P(("groups", "seq"), None, None, None),
        P(),
        P(),
        P(),
        P(),
        P("groups", "seq", None),
    )
    out_specs = (
        P("groups", "seq", None),
        P("groups", None, None, None),
        P("groups", None, None, None),
    )
    return jax.shard_map(
        functools.partial(local, mesh.shape["seq"]),
        mesh=mesh,
        in_specs=in_specs,
        out_specs=out_specs,
        check_vma=False,
    )
```

```python
import functools

import jax
import jax.numpy as jnp
from jax import lax
from jax.experimental import pallas as pl
from jax.experimental.pallas import tpu as pltpu
from jax.sharding import PartitionSpec as P

F32, BF16 = jnp.float32, jnp.bfloat16
VMEM_LIMIT = 24 * 1024 * 1024
ROWS = (((0,), (0,)), ((), ()))
VMEM = pl.BlockSpec(memory_space=pltpu.VMEM)
HBM = pl.BlockSpec(memory_space=pltpu.HBM)
SMEM = pl.BlockSpec(memory_space=pltpu.SMEM)


def dot(a, b):
    return jnp.dot(a, b, preferred_element_type=F32)


def on_chip(x):
    return pltpu.with_memory_space_constraint(x, pltpu.VMEM)


def moved_down(values, period):
    row = lax.broadcasted_iota(jnp.int32, values.shape, 0)
    return jnp.where(lax.rem(row, period) == 0, 0.0, pltpu.roll(values, 1, 0))


def moved_up(values, period):
    row = lax.broadcasted_iota(jnp.int32, values.shape, 0)
    return jnp.where(
        lax.rem(row, period) == period - 1, 0.0, pltpu.roll(values, values.shape[0] - 1, 0)
    )


def in_hbm(x):
    return pltpu.with_memory_space_constraint(x, pltpu.HBM)


def conv_kernel(x_hbm, w_hbm, out_ref, planes, buf, weights, wide, sems, w_sem, *, bands):
    count, height, width, channels = x_hbm.shape
    out_cols = width // 2
    band = height // bands
    out_band = band // 2
    copies = []
    for frame in range(count):
        for b in range(bands):
            rows = pl.ds(b * band, band)
            copies.append(
                pltpu.make_async_copy(
                    x_hbm.at[frame, rows], buf.at[frame, rows], sems.at[frame * bands + b]
                )
            )
    copies[0].start()
    w_copy = pltpu.make_async_copy(w_hbm, weights, w_sem)
    w_copy.start()
    for copy in copies[1:]:
        copy.start()
    zero = jnp.zeros((out_cols, 2 * channels), BF16)
    chunk_pixels = out_ref.shape[2]
    owners = out_band * out_cols // chunk_pixels
    for frame in range(count):
        planes[frame, 0] = zero
        for b in range(bands):
            copies[frame * bands + b].wait()
            for row in range(b * band, (b + 1) * band):
                slot = row % wide.shape[0]
                wide[slot] = buf[frame, row].astype(F32)
                even = wide[slot, pl.ds(0, out_cols, stride=2), :]
                odd = wide[slot, pl.ds(1, out_cols, stride=2), :]
                planes[frame, row + 1, :, :channels] = even.astype(BF16)
                planes[frame, row + 1, :, channels:] = odd.astype(BF16)
            if frame == 0 and b == 0:
                w_copy.wait()
                w_even = jnp.concatenate([weights[a, 1] for a in range(3)], 0)
                w_odd = jnp.concatenate(
                    [jnp.concatenate([weights[a, 2], weights[a, 0]], 1) for a in range(3)], 0
                )
            first = b * out_band

            def taps(lanes):
                return jnp.concatenate(
                    [
                        jnp.concatenate(
                            [planes[frame, 2 * i + a, :, lanes] for i in range(first, first + out_band)], 0
                        )
                        for a in range(3)
                    ],
                    1,
                )

            odds = dot(taps(slice(channels, 2 * channels)), w_odd)
            total = dot(taps(slice(0, channels)), w_even) + odds[:, :channels]
            total = (total + moved_down(odds[:, channels:], out_cols)).astype(BF16)
            out_ref[pl.ds(b * owners, owners), frame] = total.reshape(owners, chunk_pixels, channels)


def conv(frames, w_spatial, n):
    count, height, width, channels = frames.shape
    out_cols = width // 2
    bands = 4
    return pl.pallas_call(
        functools.partial(conv_kernel, bands=bands),
        in_specs=[HBM, HBM],
        out_specs=[VMEM, VMEM],
        out_shape=[
            pltpu.VMEM((n, count, height // 2 * out_cols // n, channels), BF16),
            pltpu.VMEM((count, height + 1, out_cols, 2 * channels), BF16),
        ],
        scratch_shapes=[
            pltpu.VMEM((count, height, width, channels), BF16),
            pltpu.VMEM(w_spatial.shape, BF16),
            pltpu.VMEM((4, width, channels), F32),
            pltpu.SemaphoreType.DMA((count * bands,)),
            pltpu.SemaphoreType.DMA,
        ],
        compiler_params=pltpu.CompilerParams(vmem_limit_bytes=VMEM_LIMIT),
        name="conv",
    )(in_hbm(frames), in_hbm(w_spatial))


def row_shifts(dil_ref, off_ref, length, pixels):
    layers, taps = off_ref.shape
    return [
        [
            pl.multiple_of(
                jnp.minimum(off_ref[layer, tap] * dil_ref[layer], length) * pixels, pixels
            )
            for tap in range(taps)
        ]
        for layer in range(layers)
    ]


def moved_rows(ref, layer, at, shifts, size, pixels):
    return jnp.concatenate(
        [ref[layer, pl.ds(pl.multiple_of(at + s, pixels), size), :] for s in shifts], 1
    )


def temporal_kernel(
    length, dil_ref, off_ref, start_ref, cot_ref, w_ref, feat_hbm, back_hbm, mid_hbm, dz_hbm, state, dz, act, grad, feat, back, sems
):
    layers, taps, channels = w_ref.shape[:3]
    rows = start_ref.shape[0]
    pixels = rows // length
    size = min(512, rows)
    starts = range(0, rows, size)
    shifts = row_shifts(dil_ref, off_ref, length, pixels)
    sent = []

    def send(source, target):
        sent.append(pltpu.make_async_copy(source, target, sems.at[len(sent)]))
        sent[-1].start()

    blank = jnp.zeros((rows, channels), BF16)
    for layer in range(layers):
        state[layer, pl.ds(0, rows), :] = blank
        dz[layer, pl.ds(rows, rows), :] = blank
    state[0, pl.ds(rows, rows), :] = start_ref[...]
    down = [w_ref[layer].reshape(taps * channels, channels) for layer in range(layers)]
    up = [
        jnp.concatenate([w_ref[layer, tap].T for tap in range(taps)], 0)
        for layer in range(layers)
    ]
    for layer in range(layers):
        last = layer == layers - 1
        for at in starts:
            here = pl.ds(at, size)
            moved = moved_rows(state, layer, rows + at, [-s for s in shifts[layer]], size, pixels)
            activ = jnp.tanh(dot(moved, down[layer]))
            held = state[layer, pl.ds(rows + at, size), :].astype(F32)
            following = (held + activ).astype(BF16)
            slope = 1.0 - activ * activ
            if last:
                feat[here, :] = following
                dz[layer, here, :] = (cot_ref[here, :].astype(F32) * slope).astype(BF16)
            else:
                state[layer + 1, pl.ds(rows + at, size), :] = following
                act[layer, here, :] = slope
        if last:
            send(feat, feat_hbm)
            send(dz.at[layer, pl.ds(0, rows)], dz_hbm.at[layer])
        else:
            send(state.at[layer + 1, pl.ds(rows, rows)], mid_hbm.at[layer])
    for layer in reversed(range(layers)):
        for at in starts:
            here = pl.ds(at, size)
            if layer == layers - 1:
                before = cot_ref[here, :].astype(F32)
            else:
                before = grad[here, :]
            after = before + dot(moved_rows(dz, layer, at, shifts[layer], size, pixels), up[layer])
            if layer > 0:
                grad[here, :] = after
                dz[layer - 1, here, :] = (after * act[layer - 1, here, :]).astype(BF16)
            else:
                back[here, :] = after.astype(BF16)
                send(back.at[here], back_hbm.at[here])
        if layer > 0:
            send(dz.at[layer - 1, pl.ds(0, rows)], dz_hbm.at[layer - 1])
    for copy in sent:
        copy.wait()


def temporal(start, cotangent, w_temporal, dilations, offsets, length):
    rows, channels = start.shape
    layers = w_temporal.shape[0]
    pieces = rows // min(512, rows)
    return pl.pallas_call(
        functools.partial(temporal_kernel, length),
        in_specs=[SMEM, SMEM, VMEM, VMEM, VMEM],
        out_specs=[HBM] * 4,
        out_shape=[
            pltpu.HBM((rows, channels), BF16),
            pltpu.HBM((rows, channels), BF16),
            pltpu.HBM((max(layers - 1, 1), rows, channels), BF16),
            pltpu.HBM((layers, rows, channels), BF16),
        ],
        scratch_shapes=[
            pltpu.VMEM((layers, 2 * rows, channels), BF16),
            pltpu.VMEM((layers, 2 * rows, channels), BF16),
            pltpu.VMEM((max(layers - 1, 1), rows, channels), F32),
            pltpu.VMEM((rows, channels), F32),
            pltpu.VMEM((rows, channels), BF16),
            pltpu.VMEM((rows, channels), BF16),
            pltpu.SemaphoreType.DMA((2 * layers + pieces,)),
        ],
        compiler_params=pltpu.CompilerParams(vmem_limit_bytes=VMEM_LIMIT),
        name="temporal",
    )(dilations, offsets, on_chip(start), on_chip(cotangent), on_chip(w_temporal))


def temporal_outer_kernel(length, dil_ref, off_ref, start_ref, mid_ref, dz_ref, out_ref, state):
    layers, taps, channels = out_ref.shape[:3]
    rows = start_ref.shape[0]
    pixels = rows // length
    size = min(1024, rows)
    shifts = row_shifts(dil_ref, off_ref, length, pixels)
    blank = jnp.zeros((rows, channels), BF16)
    for layer in range(layers):
        state[layer, pl.ds(0, rows), :] = blank
        held = start_ref[...] if layer == 0 else mid_ref[layer - 1]
        state[layer, pl.ds(rows, rows), :] = held
        total = jnp.zeros((channels, taps * channels), F32)
        for at in range(0, rows, size):
            moved = moved_rows(state, layer, rows + at, [-s for s in shifts[layer]], size, pixels)
            values = dz_ref[layer, pl.ds(at, size), :]
            total += lax.dot_general(values, moved, ROWS, preferred_element_type=F32)
        for tap in range(taps):
            out_ref[layer, tap] = total[:, tap * channels : (tap + 1) * channels].T


def temporal_outer(start, mid, dz, dilations, offsets, length):
    rows, channels = start.shape
    layers, taps = offsets.shape
    return pl.pallas_call(
        functools.partial(temporal_outer_kernel, length),
        in_specs=[SMEM, SMEM, VMEM, VMEM, VMEM],
        out_specs=VMEM,
        out_shape=pltpu.VMEM((layers, taps, channels, channels), F32),
        scratch_shapes=[pltpu.VMEM((layers, 2 * rows, channels), BF16)],
        compiler_params=pltpu.CompilerParams(vmem_limit_bytes=VMEM_LIMIT),
        name="temporal_outer",
    )(dilations, offsets, on_chip(start), mid, dz)


def spatial_outer_kernel(planes, back_ref, out_ref):
    count, height, out_cols, channels = planes.shape
    channels //= 2
    out_rows = (height - 1) // 2
    totals = [jnp.zeros((2 * channels, 2 * channels), F32) for _ in range(3)]
    for frame in range(count):
        back = back_ref[:, frame].reshape(out_rows * out_cols, channels)
        up = moved_up(back.astype(F32), out_cols).astype(BF16)
        both = jnp.concatenate([back, up], 1).T
        for a in range(3):
            moved = jnp.concatenate([planes[frame, 2 * i + a] for i in range(out_rows)], 0)
            totals[a] += dot(both, moved)
    for a in range(3):
        out_ref[a, 1] = totals[a][:channels, :channels].T
        out_ref[a, 2] = totals[a][:channels, channels:].T
        out_ref[a, 0] = totals[a][channels:, channels:].T


def spatial_outer(planes, back):
    channels = planes.shape[-1] // 2
    return pl.pallas_call(
        spatial_outer_kernel,
        in_specs=[VMEM, VMEM],
        out_specs=VMEM,
        out_shape=pltpu.VMEM((3, 3, channels, channels), F32),
        compiler_params=pltpu.CompilerParams(vmem_limit_bytes=VMEM_LIMIT),
        name="spatial_outer",
    )(on_chip(planes), on_chip(back))


def swap(x, n, bit):
    return lax.ppermute(x, "seq", [(i, i ^ (1 << bit)) for i in range(n)])


def sum_halves(values, n, halved):
    me = lax.axis_index("seq")
    for bit in range(halved):
        half = values.shape[0] // 2
        upper = (me >> bit) & 1
        pieces = values.reshape(2, half, -1)
        mine = lax.dynamic_index_in_dim(pieces, upper, 0, keepdims=False)
        other = lax.dynamic_index_in_dim(pieces, 1 - upper, 0, keepdims=False)
        values = mine + swap(other.astype(BF16), n, bit).astype(F32)
    return values


def sum_whole(values, n, bits):
    for bit in bits:
        sent = values.astype(BF16)
        values = sent.astype(F32) + swap(sent, n, bit).astype(F32)
    return values


def gather_halves(values, n, halved):
    me = lax.axis_index("seq")
    for bit in reversed(range(halved)):
        got = swap(values, n, bit)
        upper = (me >> bit) & 1
        values = jnp.where(upper == 0, jnp.stack([values, got]), jnp.stack([got, values]))
    return values


def exchange(x):
    return lax.all_to_all(x, "seq", split_axis=0, concat_axis=0, tiled=True)


def local(n, frames, w_spatial, w_temporal, dilations, offsets, cotangent):
    count, height, width, channels = frames.shape
    length, pixels = cotangent.shape[:2]
    bits = n.bit_length() - 1
    halved = min(2, bits)
    maps, planes = conv(frames, w_spatial, n)
    start = exchange(maps.reshape(n, count * pixels, channels)).reshape(length * pixels, channels)
    features, grad_maps, mid, dz = temporal(
        start, cotangent.reshape(length * pixels, channels), w_temporal, dilations, offsets, length
    )
    back = exchange(grad_maps.reshape(n, count * pixels, channels))
    grad_temporal = temporal_outer(start, mid, dz, dilations, offsets, length)
    of_temporal = sum_halves(grad_temporal.reshape(-1, channels), n, halved)
    grad_spatial = spatial_outer(planes, back.reshape(n, count, pixels, channels))
    of_temporal = sum_whole(of_temporal, n, range(halved, bits))
    of_temporal = gather_halves(of_temporal.astype(BF16), n, halved).astype(F32)
    of_spatial = sum_halves(grad_spatial.reshape(-1, channels), n, halved)
    of_spatial = sum_whole(of_spatial, n, range(halved, bits))
    of_spatial = gather_halves(of_spatial.astype(BF16), n, halved).astype(F32)
    return (
        features.reshape(length, pixels, channels),
        of_spatial.reshape(grad_spatial.shape),
        of_temporal.reshape(grad_temporal.shape),
    )


def solution(mesh):
    in_specs = (
        P(("groups", "seq"), None, None, None),
        P(),
        P(),
        P(),
        P(),
        P("groups", "seq", None),
    )
    out_specs = (
        P("groups", "seq", None),
        P("groups", None, None, None),
        P("groups", None, None, None),
    )
    return jax.shard_map(
        functools.partial(local, mesh.shape["seq"]),
        mesh=mesh,
        in_specs=in_specs,
        out_specs=out_specs,
        check_vma=False,
    )
```

```python
import functools

import jax
import jax.numpy as jnp
from jax import lax
from jax.experimental import pallas as pl
from jax.experimental.pallas import tpu as pltpu
from jax.sharding import PartitionSpec as P

F32, BF16 = jnp.float32, jnp.bfloat16
VMEM_LIMIT = 24 * 1024 * 1024
ROWS = (((0,), (0,)), ((), ()))
VMEM = pl.BlockSpec(memory_space=pltpu.VMEM)
HBM = pl.BlockSpec(memory_space=pltpu.HBM)
SMEM = pl.BlockSpec(memory_space=pltpu.SMEM)


def dot(a, b):
    return jnp.dot(a, b, preferred_element_type=F32)


def on_chip(x):
    return pltpu.with_memory_space_constraint(x, pltpu.VMEM)


def moved_down(values, period):
    row = lax.broadcasted_iota(jnp.int32, values.shape, 0)
    return jnp.where(lax.rem(row, period) == 0, 0.0, pltpu.roll(values, 1, 0))


def moved_up(values, period):
    row = lax.broadcasted_iota(jnp.int32, values.shape, 0)
    return jnp.where(
        lax.rem(row, period) == period - 1, 0.0, pltpu.roll(values, values.shape[0] - 1, 0)
    )


def in_hbm(x):
    return pltpu.with_memory_space_constraint(x, pltpu.HBM)


def conv_kernel(x_hbm, w_hbm, out_ref, planes, buf, weights, wide, sems, w_sem, *, bands):
    count, height, width, channels = x_hbm.shape
    out_cols = width // 2
    band = height // bands
    out_rows = height // 2
    copies = []
    for frame in range(count):
        for b in range(bands):
            rows = pl.ds(b * band, band)
            copies.append(
                pltpu.make_async_copy(
                    x_hbm.at[frame, rows], buf.at[frame, rows], sems.at[frame * bands + b]
                )
            )
    copies[0].start()
    w_copy = pltpu.make_async_copy(w_hbm, weights, w_sem)
    w_copy.start()
    for copy in copies[1:]:
        copy.start()
    zero = jnp.zeros((out_cols, 2 * channels), BF16)
    chunk_pixels = out_ref.shape[2]
    owners = out_rows * out_cols // chunk_pixels
    for frame in range(count):
        planes[frame, 0] = zero
        for b in range(bands):
            copies[frame * bands + b].wait()
            for row in range(b * band, (b + 1) * band):
                slot = row % wide.shape[0]
                wide[slot] = buf[frame, row].astype(F32)
                even = wide[slot, pl.ds(0, out_cols, stride=2), :]
                odd = wide[slot, pl.ds(1, out_cols, stride=2), :]
                planes[frame, row + 1, :, :channels] = even.astype(BF16)
                planes[frame, row + 1, :, channels:] = odd.astype(BF16)
        if frame == 0:
            w_copy.wait()
            w_even = jnp.concatenate([weights[a, 1] for a in range(3)], 0)
            w_odd = jnp.concatenate(
                [jnp.concatenate([weights[a, 2], weights[a, 0]], 1) for a in range(3)], 0
            )

        def taps(lanes):
            return jnp.concatenate(
                [
                    jnp.concatenate(
                        [planes[frame, 2 * i + a, :, lanes] for i in range(out_rows)], 0
                    )
                    for a in range(3)
                ],
                1,
            )

        odds = dot(taps(slice(channels, 2 * channels)), w_odd)
        total = dot(taps(slice(0, channels)), w_even) + odds[:, :channels]
        total = (total + moved_down(odds[:, channels:], out_cols)).astype(BF16)
        out_ref[:, frame] = total.reshape(owners, chunk_pixels, channels)


def conv(frames, w_spatial, n):
    count, height, width, channels = frames.shape
    out_cols = width // 2
    bands = 4
    return pl.pallas_call(
        functools.partial(conv_kernel, bands=bands),
        in_specs=[HBM, HBM],
        out_specs=[VMEM, VMEM],
        out_shape=[
            pltpu.VMEM((n, count, height // 2 * out_cols // n, channels), BF16),
            pltpu.VMEM((count, height + 1, out_cols, 2 * channels), BF16),
        ],
        scratch_shapes=[
            pltpu.VMEM((count, height, width, channels), BF16),
            pltpu.VMEM(w_spatial.shape, BF16),
            pltpu.VMEM((4, width, channels), F32),
            pltpu.SemaphoreType.DMA((count * bands,)),
            pltpu.SemaphoreType.DMA,
        ],
        compiler_params=pltpu.CompilerParams(vmem_limit_bytes=VMEM_LIMIT),
        name="conv",
    )(in_hbm(frames), in_hbm(w_spatial))


def row_shifts(dil_ref, off_ref, length, pixels):
    layers, taps = off_ref.shape
    return [
        [
            pl.multiple_of(
                jnp.minimum(off_ref[layer, tap] * dil_ref[layer], length) * pixels, pixels
            )
            for tap in range(taps)
        ]
        for layer in range(layers)
    ]


def moved_rows(ref, layer, at, shifts, size, pixels):
    return jnp.concatenate(
        [ref[layer, pl.ds(pl.multiple_of(at + s, pixels), size), :] for s in shifts], 1
    )


def temporal_kernel(
    length, dil_ref, off_ref, start_ref, cot_ref, w_ref, feat_hbm, back_hbm, mid_hbm, dz_hbm, state, dz, act, grad, feat, back, sems
):
    layers, taps, channels = w_ref.shape[:3]
    rows = start_ref.shape[0]
    pixels = rows // length
    size = min(1024, rows)
    starts = range(0, rows, size)
    shifts = row_shifts(dil_ref, off_ref, length, pixels)
    sent = []

    def send(source, target):
        sent.append(pltpu.make_async_copy(source, target, sems.at[len(sent)]))
        sent[-1].start()

    blank = jnp.zeros((rows, channels), BF16)
    for layer in range(layers):
        state[layer, pl.ds(0, rows), :] = blank
        dz[layer, pl.ds(rows, rows), :] = blank
    state[0, pl.ds(rows, rows), :] = start_ref[...]
    down = [w_ref[layer].reshape(taps * channels, channels) for layer in range(layers)]
    up = [
        jnp.concatenate([w_ref[layer, tap].T for tap in range(taps)], 0)
        for layer in range(layers)
    ]
    for layer in range(layers):
        last = layer == layers - 1
        for at in starts:
            here = pl.ds(at, size)
            moved = moved_rows(state, layer, rows + at, [-s for s in shifts[layer]], size, pixels)
            activ = jnp.tanh(dot(moved, down[layer]))
            held = state[layer, pl.ds(rows + at, size), :].astype(F32)
            following = (held + activ).astype(BF16)
            slope = 1.0 - activ * activ
            if last:
                feat[here, :] = following
                dz[layer, here, :] = (cot_ref[here, :].astype(F32) * slope).astype(BF16)
            else:
                state[layer + 1, pl.ds(rows + at, size), :] = following
                act[layer, here, :] = slope
        if last:
            send(feat, feat_hbm)
            send(dz.at[layer, pl.ds(0, rows)], dz_hbm.at[layer])
        else:
            send(state.at[layer + 1, pl.ds(rows, rows)], mid_hbm.at[layer])
    for layer in reversed(range(layers)):
        for at in starts:
            here = pl.ds(at, size)
            if layer == layers - 1:
                before = cot_ref[here, :].astype(F32)
            else:
                before = grad[here, :]
            after = before + dot(moved_rows(dz, layer, at, shifts[layer], size, pixels), up[layer])
            if layer > 0:
                grad[here, :] = after
                dz[layer - 1, here, :] = (after * act[layer - 1, here, :]).astype(BF16)
            else:
                back[here, :] = after.astype(BF16)
                send(back.at[here], back_hbm.at[here])
        if layer > 0:
            send(dz.at[layer - 1, pl.ds(0, rows)], dz_hbm.at[layer - 1])
    for copy in sent:
        copy.wait()


def temporal(start, cotangent, w_temporal, dilations, offsets, length):
    rows, channels = start.shape
    layers = w_temporal.shape[0]
    pieces = rows // min(1024, rows)
    return pl.pallas_call(
        functools.partial(temporal_kernel, length),
        in_specs=[SMEM, SMEM, VMEM, VMEM, VMEM],
        out_specs=[HBM] * 4,
        out_shape=[
            pltpu.HBM((rows, channels), BF16),
            pltpu.HBM((rows, channels), BF16),
            pltpu.HBM((max(layers - 1, 1), rows, channels), BF16),
            pltpu.HBM((layers, rows, channels), BF16),
        ],
        scratch_shapes=[
            pltpu.VMEM((layers, 2 * rows, channels), BF16),
            pltpu.VMEM((layers, 2 * rows, channels), BF16),
            pltpu.VMEM((max(layers - 1, 1), rows, channels), F32),
            pltpu.VMEM((rows, channels), F32),
            pltpu.VMEM((rows, channels), BF16),
            pltpu.VMEM((rows, channels), BF16),
            pltpu.SemaphoreType.DMA((2 * layers + pieces,)),
        ],
        compiler_params=pltpu.CompilerParams(vmem_limit_bytes=VMEM_LIMIT),
        name="temporal",
    )(dilations, offsets, on_chip(start), on_chip(cotangent), on_chip(w_temporal))


def temporal_outer_kernel(length, dil_ref, off_ref, start_ref, mid_ref, dz_ref, out_ref, state):
    layers, taps, channels = out_ref.shape[:3]
    rows = start_ref.shape[0]
    pixels = rows // length
    size = min(1024, rows)
    shifts = row_shifts(dil_ref, off_ref, length, pixels)
    blank = jnp.zeros((rows, channels), BF16)
    for layer in range(layers):
        state[layer, pl.ds(0, rows), :] = blank
        held = start_ref[...] if layer == 0 else mid_ref[layer - 1]
        state[layer, pl.ds(rows, rows), :] = held
        total = jnp.zeros((channels, taps * channels), F32)
        for at in range(0, rows, size):
            moved = moved_rows(state, layer, rows + at, [-s for s in shifts[layer]], size, pixels)
            values = dz_ref[layer, pl.ds(at, size), :]
            total += lax.dot_general(values, moved, ROWS, preferred_element_type=F32)
        for tap in range(taps):
            out_ref[layer, tap] = total[:, tap * channels : (tap + 1) * channels].T


def temporal_outer(start, mid, dz, dilations, offsets, length):
    rows, channels = start.shape
    layers, taps = offsets.shape
    return pl.pallas_call(
        functools.partial(temporal_outer_kernel, length),
        in_specs=[SMEM, SMEM, VMEM, VMEM, VMEM],
        out_specs=VMEM,
        out_shape=pltpu.VMEM((layers, taps, channels, channels), F32),
        scratch_shapes=[pltpu.VMEM((layers, 2 * rows, channels), BF16)],
        compiler_params=pltpu.CompilerParams(vmem_limit_bytes=VMEM_LIMIT),
        name="temporal_outer",
    )(dilations, offsets, on_chip(start), mid, dz)


def spatial_outer_kernel(planes, back_ref, out_ref):
    count, height, out_cols, channels = planes.shape
    channels //= 2
    out_rows = (height - 1) // 2
    totals = [jnp.zeros((2 * channels, 2 * channels), F32) for _ in range(3)]
    for frame in range(count):
        back = back_ref[:, frame].reshape(out_rows * out_cols, channels)
        up = moved_up(back.astype(F32), out_cols).astype(BF16)
        both = jnp.concatenate([back, up], 1).T
        for a in range(3):
            moved = jnp.concatenate([planes[frame, 2 * i + a] for i in range(out_rows)], 0)
            totals[a] += dot(both, moved)
    for a in range(3):
        out_ref[a, 1] = totals[a][:channels, :channels].T
        out_ref[a, 2] = totals[a][:channels, channels:].T
        out_ref[a, 0] = totals[a][channels:, channels:].T


def spatial_outer(planes, back):
    channels = planes.shape[-1] // 2
    return pl.pallas_call(
        spatial_outer_kernel,
        in_specs=[VMEM, VMEM],
        out_specs=VMEM,
        out_shape=pltpu.VMEM((3, 3, channels, channels), F32),
        compiler_params=pltpu.CompilerParams(vmem_limit_bytes=VMEM_LIMIT),
        name="spatial_outer",
    )(on_chip(planes), on_chip(back))


def swap(x, n, bit):
    return lax.ppermute(x, "seq", [(i, i ^ (1 << bit)) for i in range(n)])


def sum_halves(values, n, halved):
    me = lax.axis_index("seq")
    for bit in range(halved):
        half = values.shape[0] // 2
        upper = (me >> bit) & 1
        pieces = values.reshape(2, half, -1)
        mine = lax.dynamic_index_in_dim(pieces, upper, 0, keepdims=False)
        other = lax.dynamic_index_in_dim(pieces, 1 - upper, 0, keepdims=False)
        values = mine + swap(other.astype(BF16), n, bit).astype(F32)
    return values


def sum_whole(values, n, bits):
    for bit in bits:
        sent = values.astype(BF16)
        values = sent.astype(F32) + swap(sent, n, bit).astype(F32)
    return values


def gather_halves(values, n, halved):
    me = lax.axis_index("seq")
    for bit in reversed(range(halved)):
        got = swap(values, n, bit)
        upper = (me >> bit) & 1
        values = jnp.where(upper == 0, jnp.stack([values, got]), jnp.stack([got, values]))
    return values


def exchange(x):
    return lax.all_to_all(x, "seq", split_axis=0, concat_axis=0, tiled=True)


def local(n, frames, w_spatial, w_temporal, dilations, offsets, cotangent):
    count, height, width, channels = frames.shape
    length, pixels = cotangent.shape[:2]
    bits = n.bit_length() - 1
    halved = min(2, bits)
    maps, planes = conv(frames, w_spatial, n)
    start = exchange(maps.reshape(n, count * pixels, channels)).reshape(length * pixels, channels)
    features, grad_maps, mid, dz = temporal(
        start, cotangent.reshape(length * pixels, channels), w_temporal, dilations, offsets, length
    )
    back = exchange(grad_maps.reshape(n, count * pixels, channels))
    grad_temporal = temporal_outer(start, mid, dz, dilations, offsets, length)
    of_temporal = sum_halves(grad_temporal.reshape(-1, channels), n, halved)
    grad_spatial = spatial_outer(planes, back.reshape(n, count, pixels, channels))
    of_temporal = sum_whole(of_temporal, n, range(halved, bits))
    of_temporal = gather_halves(of_temporal.astype(BF16), n, halved).astype(F32)
    of_spatial = sum_halves(grad_spatial.reshape(-1, channels), n, halved)
    of_spatial = sum_whole(of_spatial, n, range(halved, bits))
    of_spatial = gather_halves(of_spatial.astype(BF16), n, halved).astype(F32)
    return (
        features.reshape(length, pixels, channels),
        of_spatial.reshape(grad_spatial.shape),
        of_temporal.reshape(grad_temporal.shape),
    )


def solution(mesh):
    in_specs = (
        P(("groups", "seq"), None, None, None),
        P(),
        P(),
        P(),
        P(),
        P("groups", "seq", None),
    )
    out_specs = (
        P("groups", "seq", None),
        P("groups", None, None, None),
        P("groups", None, None, None),
    )
    return jax.shard_map(
        functools.partial(local, mesh.shape["seq"]),
        mesh=mesh,
        in_specs=in_specs,
        out_specs=out_specs,
        check_vma=False,
    )
```

```python
import functools

import jax
import jax.numpy as jnp
from jax import lax
from jax.experimental import pallas as pl
from jax.experimental.pallas import tpu as pltpu
from jax.sharding import PartitionSpec as P

F32, BF16 = jnp.float32, jnp.bfloat16
VMEM_LIMIT = 24 * 1024 * 1024
ROWS = (((0,), (0,)), ((), ()))
VMEM = pl.BlockSpec(memory_space=pltpu.VMEM)
HBM = pl.BlockSpec(memory_space=pltpu.HBM)
SMEM = pl.BlockSpec(memory_space=pltpu.SMEM)


def dot(a, b):
    return jnp.dot(a, b, preferred_element_type=F32)


def on_chip(x):
    return pltpu.with_memory_space_constraint(x, pltpu.VMEM)


def moved_down(values, period):
    row = lax.broadcasted_iota(jnp.int32, values.shape, 0)
    return jnp.where(lax.rem(row, period) == 0, 0.0, pltpu.roll(values, 1, 0))


def moved_up(values, period):
    row = lax.broadcasted_iota(jnp.int32, values.shape, 0)
    return jnp.where(
        lax.rem(row, period) == period - 1, 0.0, pltpu.roll(values, values.shape[0] - 1, 0)
    )


def in_hbm(x):
    return pltpu.with_memory_space_constraint(x, pltpu.HBM)


def conv_kernel(x_hbm, w_hbm, out_ref, planes, buf, weights, wide, sems, w_sem, *, bands):
    count, height, width, channels = x_hbm.shape
    out_cols = width // 2
    band = height // bands
    out_rows = height // 2
    copies = []
    for frame in range(count):
        for b in range(bands):
            rows = pl.ds(b * band, band)
            copies.append(
                pltpu.make_async_copy(
                    x_hbm.at[frame, rows], buf.at[frame, rows], sems.at[frame * bands + b]
                )
            )
    copies[0].start()
    w_copy = pltpu.make_async_copy(w_hbm, weights, w_sem)
    w_copy.start()
    for copy in copies[1:]:
        copy.start()
    zero = jnp.zeros((out_cols, 2 * channels), BF16)
    chunk_pixels = out_ref.shape[2]
    owners = out_rows * out_cols // chunk_pixels
    for frame in range(count):
        planes[frame, 0] = zero
        for b in range(bands):
            copies[frame * bands + b].wait()
            for row in range(b * band, (b + 1) * band):
                slot = row % wide.shape[0]
                wide[slot] = buf[frame, row].astype(F32)
                even = wide[slot, pl.ds(0, out_cols, stride=2), :]
                odd = wide[slot, pl.ds(1, out_cols, stride=2), :]
                planes[frame, row + 1, :, :channels] = even.astype(BF16)
                planes[frame, row + 1, :, channels:] = odd.astype(BF16)
        if frame == 0:
            w_copy.wait()
            w_even = jnp.concatenate([weights[a, 1] for a in range(3)], 0)
            w_odd = jnp.concatenate(
                [jnp.concatenate([weights[a, 2], weights[a, 0]], 1) for a in range(3)], 0
            )

        def taps(lanes):
            return jnp.concatenate(
                [
                    jnp.concatenate(
                        [planes[frame, 2 * i + a, :, lanes] for i in range(out_rows)], 0
                    )
                    for a in range(3)
                ],
                1,
            )

        odds = dot(taps(slice(channels, 2 * channels)), w_odd)
        total = dot(taps(slice(0, channels)), w_even) + odds[:, :channels]
        total = (total + moved_down(odds[:, channels:], out_cols)).astype(BF16)
        out_ref[:, frame] = total.reshape(owners, chunk_pixels, channels)


def conv(frames, w_spatial, n):
    count, height, width, channels = frames.shape
    out_cols = width // 2
    bands = 4
    return pl.pallas_call(
        functools.partial(conv_kernel, bands=bands),
        in_specs=[HBM, HBM],
        out_specs=[VMEM, VMEM],
        out_shape=[
            pltpu.VMEM((n, count, height // 2 * out_cols // n, channels), BF16),
            pltpu.VMEM((count, height + 1, out_cols, 2 * channels), BF16),
        ],
        scratch_shapes=[
            pltpu.VMEM((count, height, width, channels), BF16),
            pltpu.VMEM(w_spatial.shape, BF16),
            pltpu.VMEM((4, width, channels), F32),
            pltpu.SemaphoreType.DMA((count * bands,)),
            pltpu.SemaphoreType.DMA,
        ],
        compiler_params=pltpu.CompilerParams(vmem_limit_bytes=VMEM_LIMIT),
        name="conv",
    )(in_hbm(frames), in_hbm(w_spatial))


def row_shifts(dil_ref, off_ref, length, pixels):
    layers, taps = off_ref.shape
    return [
        [
            pl.multiple_of(
                jnp.minimum(off_ref[layer, tap] * dil_ref[layer], length) * pixels, pixels
            )
            for tap in range(taps)
        ]
        for layer in range(layers)
    ]


def moved_rows(ref, layer, at, shifts, size, pixels):
    return jnp.concatenate(
        [ref[layer, pl.ds(pl.multiple_of(at + s, pixels), size), :] for s in shifts], 1
    )


def temporal_kernel(
    length, dil_ref, off_ref, start_ref, cot_ref, w_ref, feat_hbm, back_hbm, mid_hbm, dz_hbm, state, dz, act, grad, feat, back, sems
):
    layers, taps, channels = w_ref.shape[:3]
    rows = start_ref.shape[0]
    pixels = rows // length
    size = min(1024, rows)
    starts = range(0, rows, size)
    shifts = row_shifts(dil_ref, off_ref, length, pixels)
    sent = []

    def send(source, target):
        sent.append(pltpu.make_async_copy(source, target, sems.at[len(sent)]))
        sent[-1].start()

    blank = jnp.zeros((rows, channels), BF16)
    for layer in range(layers):
        state[layer, pl.ds(0, rows), :] = blank
        dz[layer, pl.ds(rows, rows), :] = blank
    state[0, pl.ds(rows, rows), :] = start_ref[...]
    down = [w_ref[layer].reshape(taps * channels, channels) for layer in range(layers)]
    up = [
        jnp.concatenate([w_ref[layer, tap].T for tap in range(taps)], 0)
        for layer in range(layers)
    ]
    for layer in range(layers):
        last = layer == layers - 1
        for at in starts:
            here = pl.ds(at, size)
            moved = moved_rows(state, layer, rows + at, [-s for s in shifts[layer]], size, pixels)
            activ = jnp.tanh(dot(moved, down[layer]))
            held = state[layer, pl.ds(rows + at, size), :].astype(F32)
            following = (held + activ).astype(BF16)
            slope = 1.0 - activ * activ
            if last:
                feat[here, :] = following
                dz[layer, here, :] = (cot_ref[here, :].astype(F32) * slope).astype(BF16)
            else:
                state[layer + 1, pl.ds(rows + at, size), :] = following
                act[layer, here, :] = slope
        if last:
            send(feat, feat_hbm)
            send(dz.at[layer, pl.ds(0, rows)], dz_hbm.at[layer])
        else:
            send(state.at[layer + 1, pl.ds(rows, rows)], mid_hbm.at[layer])
    for layer in reversed(range(layers)):
        for at in starts:
            here = pl.ds(at, size)
            if layer == layers - 1:
                before = cot_ref[here, :].astype(F32)
            else:
                before = grad[here, :]
            after = before + dot(moved_rows(dz, layer, at, shifts[layer], size, pixels), up[layer])
            if layer > 0:
                grad[here, :] = after
                dz[layer - 1, here, :] = (after * act[layer - 1, here, :]).astype(BF16)
            else:
                back[here, :] = after.astype(BF16)
                send(back.at[here], back_hbm.at[here])
        if layer > 0:
            send(dz.at[layer - 1, pl.ds(0, rows)], dz_hbm.at[layer - 1])
    for copy in sent:
        copy.wait()


def temporal(start, cotangent, w_temporal, dilations, offsets, length):
    rows, channels = start.shape
    layers = w_temporal.shape[0]
    pieces = rows // min(1024, rows)
    return pl.pallas_call(
        functools.partial(temporal_kernel, length),
        in_specs=[SMEM, SMEM, VMEM, VMEM, VMEM],
        out_specs=[HBM] * 4,
        out_shape=[
            pltpu.HBM((rows, channels), BF16),
            pltpu.HBM((rows, channels), BF16),
            pltpu.HBM((max(layers - 1, 1), rows, channels), BF16),
            pltpu.HBM((layers, rows, channels), BF16),
        ],
        scratch_shapes=[
            pltpu.VMEM((layers, 2 * rows, channels), BF16),
            pltpu.VMEM((layers, 2 * rows, channels), BF16),
            pltpu.VMEM((max(layers - 1, 1), rows, channels), F32),
            pltpu.VMEM((rows, channels), F32),
            pltpu.VMEM((rows, channels), BF16),
            pltpu.VMEM((rows, channels), BF16),
            pltpu.SemaphoreType.DMA((2 * layers + pieces,)),
        ],
        compiler_params=pltpu.CompilerParams(vmem_limit_bytes=VMEM_LIMIT),
        name="temporal",
    )(dilations, offsets, on_chip(start), on_chip(cotangent), on_chip(w_temporal))


def deal(core_ref, whole, own_ref, other_ref):
    half = own_ref.shape[0]
    core = core_ref[0]
    own_ref[...] = whole[pl.ds(pl.multiple_of(core * half, half), half), :]
    other_ref[...] = whole[pl.ds(pl.multiple_of((1 - core) * half, half), half), :].astype(BF16)


def temporal_outer_kernel(
    length, core_ref, dil_ref, off_ref, start_ref, mid_hbm, dz_hbm, own_ref, other_ref, state, dz, whole, sems
):
    layers, taps = off_ref.shape
    rows, channels = start_ref.shape
    pixels = rows // length
    size = min(1024, rows)
    copies = []
    for layer in range(layers):
        copies.append([pltpu.make_async_copy(dz_hbm.at[layer], dz.at[layer], sems.at[2 * layer])])
        if layer > 0:
            target = state.at[layer, pl.ds(rows, rows)]
            copies[-1].append(
                pltpu.make_async_copy(mid_hbm.at[layer - 1], target, sems.at[2 * layer + 1])
            )
        for copy in copies[-1]:
            copy.start()
    shifts = row_shifts(dil_ref, off_ref, length, pixels)
    blank = jnp.zeros((rows, channels), BF16)
    for layer in range(layers):
        state[layer, pl.ds(0, rows), :] = blank
        if layer == 0:
            state[layer, pl.ds(rows, rows), :] = start_ref[...]
        for copy in copies[layer]:
            copy.wait()
        total = jnp.zeros((channels, taps * channels), F32)
        for at in range(0, rows, size):
            moved = moved_rows(state, layer, rows + at, [-s for s in shifts[layer]], size, pixels)
            values = dz[layer, pl.ds(at, size), :]
            total += lax.dot_general(values, moved, ROWS, preferred_element_type=F32)
        for tap in range(taps):
            place = pl.ds((layer * taps + tap) * channels, channels)
            whole[place, :] = total[:, tap * channels : (tap + 1) * channels].T
    deal(core_ref, whole, own_ref, other_ref)


def temporal_outer(start, mid, dz, dilations, offsets, length, core):
    rows, channels = start.shape
    layers, taps = offsets.shape
    half = layers * taps * channels // 2
    return pl.pallas_call(
        functools.partial(temporal_outer_kernel, length),
        in_specs=[SMEM, SMEM, SMEM, VMEM, HBM, HBM],
        out_specs=[VMEM, VMEM],
        out_shape=[pltpu.VMEM((half, channels), F32), pltpu.VMEM((half, channels), BF16)],
        scratch_shapes=[
            pltpu.VMEM((layers, 2 * rows, channels), BF16),
            pltpu.VMEM((layers, rows, channels), BF16),
            pltpu.VMEM((2 * half, channels), F32),
            pltpu.SemaphoreType.DMA((2 * layers,)),
        ],
        compiler_params=pltpu.CompilerParams(vmem_limit_bytes=VMEM_LIMIT),
        name="temporal_outer",
    )(core, dilations, offsets, on_chip(start), in_hbm(mid), in_hbm(dz))


def spatial_outer_kernel(core_ref, planes, back_ref, own_ref, other_ref, whole):
    count, height, out_cols, channels = planes.shape
    channels //= 2
    out_rows = (height - 1) // 2
    totals = [jnp.zeros((2 * channels, 2 * channels), F32) for _ in range(3)]
    for frame in range(count):
        back = back_ref[:, frame].reshape(out_rows * out_cols, channels)
        up = moved_up(back.astype(F32), out_cols).astype(BF16)
        both = jnp.concatenate([back, up], 1).T
        for a in range(3):
            moved = jnp.concatenate([planes[frame, 2 * i + a] for i in range(out_rows)], 0)
            totals[a] += dot(both, moved)
    for a in range(3):
        products = (
            totals[a][channels:, channels:],
            totals[a][:channels, :channels],
            totals[a][:channels, channels:],
        )
        for b, product in enumerate(products):
            whole[pl.ds((3 * a + b) * channels, channels), :] = product.T
    deal(core_ref, whole, own_ref, other_ref)


def spatial_outer(planes, back, core):
    channels = planes.shape[-1] // 2
    half = 9 * channels // 2
    return pl.pallas_call(
        spatial_outer_kernel,
        in_specs=[SMEM, VMEM, VMEM],
        out_specs=[VMEM, VMEM],
        out_shape=[pltpu.VMEM((half, channels), F32), pltpu.VMEM((half, channels), BF16)],
        scratch_shapes=[pltpu.VMEM((2 * half, channels), F32)],
        compiler_params=pltpu.CompilerParams(vmem_limit_bytes=VMEM_LIMIT),
        name="spatial_outer",
    )(core, on_chip(planes), on_chip(back))


def swap(x, n, mask):
    return lax.ppermute(x, "seq", [(i, i ^ mask) for i in range(n)])


def sum_parts(values, n, low, count):
    me = lax.rem(lax.axis_index("seq") >> low, 1 << count)
    parts = values.reshape(1 << count, values.shape[0] >> count, -1)
    total = lax.dynamic_index_in_dim(parts, me, 0, keepdims=False)
    for peer in range(1, 1 << count):
        theirs = lax.dynamic_index_in_dim(parts, me ^ peer, 0, keepdims=False)
        total = total + swap(theirs.astype(BF16), n, peer << low).astype(F32)
    return total


def sum_whole(values, n, bits):
    for bit in bits:
        sent = values.astype(BF16)
        values = sent.astype(F32) + swap(sent, n, 1 << bit).astype(F32)
    return values


def gather_parts(values, n, low, count):
    me = lax.axis_index("seq") >> low
    held = [values] + [swap(values, n, peer << low) for peer in range(1, 1 << count)]
    for bit in range(count):
        upper = (me >> bit) & 1
        step = 1 << bit
        held = [jnp.where(upper == 0, held[q], held[q ^ step]) for q in range(1 << count)]
    return jnp.concatenate(held, 0)


def widen_kernel(core_ref, own_ref, got_ref, spatial_ref, temporal_ref):
    cut = spatial_ref.shape[2]
    core = core_ref[0]
    for place, ref in ((core, own_ref), (1 - core, got_ref)):
        spatial_ref[place] = ref[:, :cut].astype(F32)
        temporal_ref[place] = ref[:, cut:].astype(F32)


def widen(own, n, core, spatial_rows, temporal_rows):
    own = own.reshape(-1, spatial_rows + temporal_rows, own.shape[-1])
    parts, channels = own.shape[0], own.shape[-1]
    return pl.pallas_call(
        widen_kernel,
        in_specs=[SMEM, VMEM, VMEM],
        out_specs=[VMEM, VMEM],
        out_shape=[
            jax.ShapeDtypeStruct((2, parts, spatial_rows, channels), F32),
            jax.ShapeDtypeStruct((2, parts, temporal_rows, channels), F32),
        ],
        compiler_params=pltpu.CompilerParams(vmem_limit_bytes=VMEM_LIMIT),
        name="widen",
    )(core, on_chip(own), on_chip(swap(own, n, 1)))


def exchange(x):
    return lax.all_to_all(x, "seq", split_axis=0, concat_axis=0, tiled=True)


def local(n, frames, w_spatial, w_temporal, dilations, offsets, cotangent):
    count, height, width, channels = frames.shape
    length, pixels = cotangent.shape[:2]
    bits = n.bit_length() - 1
    maps, planes = conv(frames, w_spatial, n)
    start = exchange(maps.reshape(n, count * pixels, channels)).reshape(length * pixels, channels)
    features, grad_maps, mid, dz = temporal(
        start, cotangent.reshape(length * pixels, channels), w_temporal, dilations, offsets, length
    )
    back = exchange(grad_maps.reshape(n, count * pixels, channels))
    core = lax.rem(lax.axis_index("seq"), 2).astype(jnp.int32).reshape(1)
    size = min(2, bits - 1)
    one = min(1, bits - 1)

    def add_cores(own, other):
        return own + swap(other, n, 1).astype(F32)

    of_temporal = sum_parts(add_cores(*temporal_outer(start, mid, dz, dilations, offsets, length, core)), n, 1, one)
    of_temporal = sum_whole(of_temporal, n, range(1 + one, min(2 + one, bits)))
    own, other = spatial_outer(planes, back.reshape(n, count, pixels, channels), core)
    of_spatial = add_cores(own, other)
    of_spatial, of_temporal = lax.optimization_barrier((of_spatial, of_temporal))
    of_spatial = sum_parts(of_spatial, n, 1, size)
    of_temporal = sum_whole(of_temporal, n, range(min(2 + one, bits), bits)).astype(BF16)
    of_temporal = gather_parts(gather_parts(of_temporal, n, 1, one), n, 0, 1)
    of_temporal = of_temporal.astype(F32).reshape(w_temporal.shape)
    of_spatial = sum_whole(of_spatial, n, range(1 + size, bits)).astype(BF16)
    of_spatial = gather_parts(gather_parts(of_spatial, n, 1, size), n, 0, 1)
    of_spatial = of_spatial.astype(F32).reshape(w_spatial.shape)
    return (
        features.reshape(length, pixels, channels),
        of_spatial.reshape(w_spatial.shape),
        of_temporal.reshape(w_temporal.shape),
    )


def solution(mesh):
    in_specs = (
        P(("groups", "seq"), None, None, None),
        P(),
        P(),
        P(),
        P(),
        P("groups", "seq", None),
    )
    out_specs = (
        P("groups", "seq", None),
        P("groups", None, None, None),
        P("groups", None, None, None),
    )
    return jax.shard_map(
        functools.partial(local, mesh.shape["seq"]),
        mesh=mesh,
        in_specs=in_specs,
        out_specs=out_specs,
        check_vma=False,
    )
```

```python
import functools

import jax
import jax.numpy as jnp
from jax import lax
from jax.experimental import pallas as pl
from jax.experimental.pallas import tpu as pltpu
from jax.sharding import PartitionSpec as P

F32, BF16 = jnp.float32, jnp.bfloat16
VMEM_LIMIT = 24 * 1024 * 1024
ROWS = (((0,), (0,)), ((), ()))
VMEM = pl.BlockSpec(memory_space=pltpu.VMEM)
HBM = pl.BlockSpec(memory_space=pltpu.HBM)
SMEM = pl.BlockSpec(memory_space=pltpu.SMEM)


def dot(a, b):
    return jnp.dot(a, b, preferred_element_type=F32)


def on_chip(x):
    return pltpu.with_memory_space_constraint(x, pltpu.VMEM)


def moved_down(values, period):
    row = lax.broadcasted_iota(jnp.int32, values.shape, 0)
    return jnp.where(lax.rem(row, period) == 0, 0.0, pltpu.roll(values, 1, 0))


def moved_up(values, period):
    row = lax.broadcasted_iota(jnp.int32, values.shape, 0)
    return jnp.where(
        lax.rem(row, period) == period - 1, 0.0, pltpu.roll(values, values.shape[0] - 1, 0)
    )


def in_hbm(x):
    return pltpu.with_memory_space_constraint(x, pltpu.HBM)


def conv_kernel(x_hbm, w_hbm, out_ref, planes, buf, weights, wide, sems, w_sem, *, bands):
    count, height, width, channels = x_hbm.shape
    out_cols = width // 2
    band = height // bands
    out_rows = height // 2
    copies = []
    for frame in range(count):
        for b in range(bands):
            rows = pl.ds(b * band, band)
            copies.append(
                pltpu.make_async_copy(
                    x_hbm.at[frame, rows], buf.at[frame, rows], sems.at[frame * bands + b]
                )
            )
    copies[0].start()
    w_copy = pltpu.make_async_copy(w_hbm, weights, w_sem)
    w_copy.start()
    for copy in copies[1:]:
        copy.start()
    zero = jnp.zeros((out_cols, 2 * channels), BF16)
    chunk_pixels = out_ref.shape[2]
    owners = out_rows * out_cols // chunk_pixels
    for frame in range(count):
        planes[frame, 0] = zero
        for b in range(bands):
            copies[frame * bands + b].wait()
            for row in range(b * band, (b + 1) * band):
                slot = row % wide.shape[0]
                wide[slot] = buf[frame, row].astype(F32)
                even = wide[slot, pl.ds(0, out_cols, stride=2), :]
                odd = wide[slot, pl.ds(1, out_cols, stride=2), :]
                planes[frame, row + 1, :, :channels] = even.astype(BF16)
                planes[frame, row + 1, :, channels:] = odd.astype(BF16)
        if frame == 0:
            w_copy.wait()
            w_even = jnp.concatenate([weights[a, 1] for a in range(3)], 0)
            w_odd = jnp.concatenate(
                [jnp.concatenate([weights[a, 2], weights[a, 0]], 1) for a in range(3)], 0
            )

        def taps(lanes):
            return jnp.concatenate(
                [
                    jnp.concatenate(
                        [planes[frame, 2 * i + a, :, lanes] for i in range(out_rows)], 0
                    )
                    for a in range(3)
                ],
                1,
            )

        odds = dot(taps(slice(channels, 2 * channels)), w_odd)
        total = dot(taps(slice(0, channels)), w_even) + odds[:, :channels]
        total = (total + moved_down(odds[:, channels:], out_cols)).astype(BF16)
        out_ref[:, frame] = total.reshape(owners, chunk_pixels, channels)


def conv(frames, w_spatial, n):
    count, height, width, channels = frames.shape
    out_cols = width // 2
    bands = 4
    return pl.pallas_call(
        functools.partial(conv_kernel, bands=bands),
        in_specs=[HBM, HBM],
        out_specs=[VMEM, VMEM],
        out_shape=[
            pltpu.VMEM((n, count, height // 2 * out_cols // n, channels), BF16),
            pltpu.VMEM((count, height + 1, out_cols, 2 * channels), BF16),
        ],
        scratch_shapes=[
            pltpu.VMEM((count, height, width, channels), BF16),
            pltpu.VMEM(w_spatial.shape, BF16),
            pltpu.VMEM((4, width, channels), F32),
            pltpu.SemaphoreType.DMA((count * bands,)),
            pltpu.SemaphoreType.DMA,
        ],
        compiler_params=pltpu.CompilerParams(vmem_limit_bytes=VMEM_LIMIT),
        name="conv",
    )(in_hbm(frames), in_hbm(w_spatial))


def row_shifts(dil_ref, off_ref, length, pixels):
    layers, taps = off_ref.shape
    return [
        [
            pl.multiple_of(
                jnp.minimum(off_ref[layer, tap] * dil_ref[layer], length) * pixels, pixels
            )
            for tap in range(taps)
        ]
        for layer in range(layers)
    ]


def moved_rows(ref, at, shifts, size, pixels):
    return jnp.concatenate(
        [ref[pl.ds(pl.multiple_of(at + s, pixels), size), :] for s in shifts], 1
    )


def temporal_kernel(
    length, dil_ref, off_ref, start_ref, cot_ref, w_ref, feat_hbm, back_hbm, mid_hbm, dz_hbm, *scratch
):
    layers, taps, channels = w_ref.shape[:3]
    state, dz = scratch[:layers], scratch[layers : 2 * layers]
    act, grad, feat, back, sems = scratch[2 * layers :]
    rows = start_ref.shape[0]
    pixels = rows // length
    size = min(1024, rows)
    starts = range(0, rows, size)
    shifts = row_shifts(dil_ref, off_ref, length, pixels)
    sent = []

    def send(source, target):
        sent.append(pltpu.make_async_copy(source, target, sems.at[len(sent)]))
        sent[-1].start()

    blank = jnp.zeros((rows, channels), BF16)
    for layer in range(layers):
        state[layer][pl.ds(0, rows), :] = blank
        dz[layer][pl.ds(rows, rows), :] = blank
    state[0][pl.ds(rows, rows), :] = start_ref[...]
    down = [w_ref[layer].reshape(taps * channels, channels) for layer in range(layers)]
    up = [
        jnp.concatenate([w_ref[layer, tap].T for tap in range(taps)], 0)
        for layer in range(layers)
    ]
    for layer in range(layers):
        last = layer == layers - 1
        for at in starts:
            here = pl.ds(at, size)
            moved = moved_rows(state[layer], rows + at, [-s for s in shifts[layer]], size, pixels)
            activ = jnp.tanh(dot(moved, down[layer]))
            held = state[layer][pl.ds(rows + at, size), :].astype(F32)
            following = (held + activ).astype(BF16)
            slope = 1.0 - activ * activ
            if last:
                feat[here, :] = following
                dz[layer][here, :] = (cot_ref[here, :].astype(F32) * slope).astype(BF16)
            else:
                state[layer + 1][pl.ds(rows + at, size), :] = following
                act[layer, here, :] = slope
        if last:
            send(feat, feat_hbm)
            send(dz[layer].at[pl.ds(0, rows)], dz_hbm.at[layer])
        else:
            send(state[layer + 1].at[pl.ds(rows, rows)], mid_hbm.at[layer])
    for layer in reversed(range(layers)):
        for at in starts:
            here = pl.ds(at, size)
            if layer == layers - 1:
                before = cot_ref[here, :].astype(F32)
            else:
                before = grad[here, :]
            after = before + dot(moved_rows(dz[layer], at, shifts[layer], size, pixels), up[layer])
            if layer > 0:
                grad[here, :] = after
                dz[layer - 1][here, :] = (after * act[layer - 1, here, :]).astype(BF16)
            else:
                back[here, :] = after.astype(BF16)
                send(back.at[here], back_hbm.at[here])
        if layer > 0:
            send(dz[layer - 1].at[pl.ds(0, rows)], dz_hbm.at[layer - 1])
    for copy in sent:
        copy.wait()


def temporal(start, cotangent, w_temporal, dilations, offsets, length):
    rows, channels = start.shape
    layers = w_temporal.shape[0]
    pieces = rows // min(1024, rows)
    return pl.pallas_call(
        functools.partial(temporal_kernel, length),
        in_specs=[SMEM, SMEM, VMEM, VMEM, VMEM],
        out_specs=[HBM] * 4,
        out_shape=[
            pltpu.HBM((rows, channels), BF16),
            pltpu.HBM((rows, channels), BF16),
            pltpu.HBM((max(layers - 1, 1), rows, channels), BF16),
            pltpu.HBM((layers, rows, channels), BF16),
        ],
        scratch_shapes=[pltpu.VMEM((2 * rows, channels), BF16)] * (2 * layers)
        + [
            pltpu.VMEM((max(layers - 1, 1), rows, channels), F32),
            pltpu.VMEM((rows, channels), F32),
            pltpu.VMEM((rows, channels), BF16),
            pltpu.VMEM((rows, channels), BF16),
            pltpu.SemaphoreType.DMA((2 * layers + pieces,)),
        ],
        compiler_params=pltpu.CompilerParams(vmem_limit_bytes=VMEM_LIMIT),
        name="temporal",
    )(dilations, offsets, on_chip(start), on_chip(cotangent), on_chip(w_temporal))


def deal(core_ref, whole, own_ref, other_ref):
    half = own_ref.shape[0]
    core = core_ref[0]
    own_ref[...] = whole[pl.ds(pl.multiple_of(core * half, half), half), :]
    other_ref[...] = whole[pl.ds(pl.multiple_of((1 - core) * half, half), half), :].astype(BF16)


def temporal_outer_kernel(
    length, core_ref, dil_ref, off_ref, start_ref, mid_hbm, dz_hbm, own_ref, other_ref, state, dz, whole, sems
):
    layers, taps = off_ref.shape
    rows, channels = start_ref.shape
    pixels = rows // length
    size = min(1024, rows)
    copies = []
    for layer in range(layers):
        copies.append([pltpu.make_async_copy(dz_hbm.at[layer], dz.at[layer], sems.at[2 * layer])])
        if layer > 0:
            target = state.at[layer, pl.ds(rows, rows)]
            copies[-1].append(
                pltpu.make_async_copy(mid_hbm.at[layer - 1], target, sems.at[2 * layer + 1])
            )
        for copy in copies[-1]:
            copy.start()
    shifts = row_shifts(dil_ref, off_ref, length, pixels)
    blank = jnp.zeros((rows, channels), BF16)
    for layer in range(layers):
        state[layer, pl.ds(0, rows), :] = blank
        if layer == 0:
            state[layer, pl.ds(rows, rows), :] = start_ref[...]
        for copy in copies[layer]:
            copy.wait()
        total = jnp.zeros((channels, taps * channels), F32)
        for at in range(0, rows, size):
            moved = moved_rows(state.at[layer], rows + at, [-s for s in shifts[layer]], size, pixels)
            values = dz[layer, pl.ds(at, size), :]
            total += lax.dot_general(values, moved, ROWS, preferred_element_type=F32)
        for tap in range(taps):
            place = pl.ds((layer * taps + tap) * channels, channels)
            whole[place, :] = total[:, tap * channels : (tap + 1) * channels].T
    deal(core_ref, whole, own_ref, other_ref)


def temporal_outer(start, mid, dz, dilations, offsets, length, core):
    rows, channels = start.shape
    layers, taps = offsets.shape
    half = layers * taps * channels // 2
    return pl.pallas_call(
        functools.partial(temporal_outer_kernel, length),
        in_specs=[SMEM, SMEM, SMEM, VMEM, HBM, HBM],
        out_specs=[VMEM, VMEM],
        out_shape=[pltpu.VMEM((half, channels), F32), pltpu.VMEM((half, channels), BF16)],
        scratch_shapes=[
            pltpu.VMEM((layers, 2 * rows, channels), BF16),
            pltpu.VMEM((layers, rows, channels), BF16),
            pltpu.VMEM((2 * half, channels), F32),
            pltpu.SemaphoreType.DMA((2 * layers,)),
        ],
        compiler_params=pltpu.CompilerParams(vmem_limit_bytes=VMEM_LIMIT),
        name="temporal_outer",
    )(core, dilations, offsets, on_chip(start), in_hbm(mid), in_hbm(dz))


def spatial_outer_kernel(core_ref, planes, back_ref, own_ref, other_ref, whole):
    count, height, out_cols, channels = planes.shape
    channels //= 2
    out_rows = (height - 1) // 2
    totals = [jnp.zeros((2 * channels, 2 * channels), F32) for _ in range(3)]
    for frame in range(count):
        back = back_ref[:, frame].reshape(out_rows * out_cols, channels)
        up = moved_up(back.astype(F32), out_cols).astype(BF16)
        both = jnp.concatenate([back, up], 1).T
        for a in range(3):
            moved = jnp.concatenate([planes[frame, 2 * i + a] for i in range(out_rows)], 0)
            totals[a] += dot(both, moved)
    for a in range(3):
        products = (
            totals[a][channels:, channels:],
            totals[a][:channels, :channels],
            totals[a][:channels, channels:],
        )
        for b, product in enumerate(products):
            whole[pl.ds((3 * a + b) * channels, channels), :] = product.T
    deal(core_ref, whole, own_ref, other_ref)


def spatial_outer(planes, back, core):
    channels = planes.shape[-1] // 2
    half = 9 * channels // 2
    return pl.pallas_call(
        spatial_outer_kernel,
        in_specs=[SMEM, VMEM, VMEM],
        out_specs=[VMEM, VMEM],
        out_shape=[pltpu.VMEM((half, channels), F32), pltpu.VMEM((half, channels), BF16)],
        scratch_shapes=[pltpu.VMEM((2 * half, channels), F32)],
        compiler_params=pltpu.CompilerParams(vmem_limit_bytes=VMEM_LIMIT),
        name="spatial_outer",
    )(core, on_chip(planes), on_chip(back))


def swap(x, n, mask):
    return lax.ppermute(x, "seq", [(i, i ^ mask) for i in range(n)])


def sum_parts(values, n, low, count):
    me = lax.rem(lax.axis_index("seq") >> low, 1 << count)
    parts = values.reshape(1 << count, values.shape[0] >> count, -1)
    total = lax.dynamic_index_in_dim(parts, me, 0, keepdims=False)
    for peer in range(1, 1 << count):
        theirs = lax.dynamic_index_in_dim(parts, me ^ peer, 0, keepdims=False)
        total = total + swap(theirs.astype(BF16), n, peer << low).astype(F32)
    return total


def sum_whole(values, n, bits):
    for bit in bits:
        sent = values.astype(BF16)
        values = sent.astype(F32) + swap(sent, n, 1 << bit).astype(F32)
    return values


def gather_parts(values, n, low, count):
    me = lax.axis_index("seq") >> low
    held = [values] + [swap(values, n, peer << low) for peer in range(1, 1 << count)]
    for bit in range(count):
        upper = (me >> bit) & 1
        step = 1 << bit
        held = [jnp.where(upper == 0, held[q], held[q ^ step]) for q in range(1 << count)]
    return jnp.concatenate(held, 0)


def widen_kernel(core_ref, own_ref, got_ref, spatial_ref, temporal_ref):
    cut = spatial_ref.shape[2]
    core = core_ref[0]
    for place, ref in ((core, own_ref), (1 - core, got_ref)):
        spatial_ref[place] = ref[:, :cut].astype(F32)
        temporal_ref[place] = ref[:, cut:].astype(F32)


def widen(own, n, core, spatial_rows, temporal_rows):
    own = own.reshape(-1, spatial_rows + temporal_rows, own.shape[-1])
    parts, channels = own.shape[0], own.shape[-1]
    return pl.pallas_call(
        widen_kernel,
        in_specs=[SMEM, VMEM, VMEM],
        out_specs=[VMEM, VMEM],
        out_shape=[
            jax.ShapeDtypeStruct((2, parts, spatial_rows, channels), F32),
            jax.ShapeDtypeStruct((2, parts, temporal_rows, channels), F32),
        ],
        compiler_params=pltpu.CompilerParams(vmem_limit_bytes=VMEM_LIMIT),
        name="widen",
    )(core, on_chip(own), on_chip(swap(own, n, 1)))


def exchange(x):
    return lax.all_to_all(x, "seq", split_axis=0, concat_axis=0, tiled=True)


def local(n, frames, w_spatial, w_temporal, dilations, offsets, cotangent):
    count, height, width, channels = frames.shape
    length, pixels = cotangent.shape[:2]
    bits = n.bit_length() - 1
    maps, planes = conv(frames, w_spatial, n)
    start = exchange(maps.reshape(n, count * pixels, channels)).reshape(length * pixels, channels)
    features, grad_maps, mid, dz = temporal(
        start, cotangent.reshape(length * pixels, channels), w_temporal, dilations, offsets, length
    )
    back = exchange(grad_maps.reshape(n, count * pixels, channels))
    core = lax.rem(lax.axis_index("seq"), 2).astype(jnp.int32).reshape(1)
    size = min(2, bits - 1)
    one = min(1, bits - 1)

    def add_cores(own, other):
        return own + swap(other, n, 1).astype(F32)

    of_temporal = sum_parts(add_cores(*temporal_outer(start, mid, dz, dilations, offsets, length, core)), n, 1, one)
    of_temporal = sum_whole(of_temporal, n, range(1 + one, min(2 + one, bits)))
    own, other = spatial_outer(planes, back.reshape(n, count, pixels, channels), core)
    of_spatial = add_cores(own, other)
    of_spatial, of_temporal = lax.optimization_barrier((of_spatial, of_temporal))
    of_spatial = sum_parts(of_spatial, n, 1, size)
    of_temporal = sum_whole(of_temporal, n, range(min(2 + one, bits), bits)).astype(BF16)
    of_temporal = gather_parts(gather_parts(of_temporal, n, 1, one), n, 0, 1)
    of_temporal = of_temporal.astype(F32).reshape(w_temporal.shape)
    of_spatial = sum_whole(of_spatial, n, range(1 + size, bits)).astype(BF16)
    of_spatial = gather_parts(gather_parts(of_spatial, n, 1, size), n, 0, 1)
    of_spatial = of_spatial.astype(F32).reshape(w_spatial.shape)
    return (
        features.reshape(length, pixels, channels),
        of_spatial.reshape(w_spatial.shape),
        of_temporal.reshape(w_temporal.shape),
    )


def solution(mesh):
    in_specs = (
        P(("groups", "seq"), None, None, None),
        P(),
        P(),
        P(),
        P(),
        P("groups", "seq", None),
    )
    out_specs = (
        P("groups", "seq", None),
        P("groups", None, None, None),
        P("groups", None, None, None),
    )
    return jax.shard_map(
        functools.partial(local, mesh.shape["seq"]),
        mesh=mesh,
        in_specs=in_specs,
        out_specs=out_specs,
        check_vma=False,
    )
```

```python
import functools

import jax
import jax.numpy as jnp
from jax import lax
from jax.experimental import pallas as pl
from jax.experimental.pallas import tpu as pltpu
from jax.sharding import PartitionSpec as P

F32, BF16 = jnp.float32, jnp.bfloat16
VMEM_LIMIT = 24 * 1024 * 1024
ROWS = (((0,), (0,)), ((), ()))
VMEM = pl.BlockSpec(memory_space=pltpu.VMEM)
HBM = pl.BlockSpec(memory_space=pltpu.HBM)
SMEM = pl.BlockSpec(memory_space=pltpu.SMEM)


def dot(a, b):
    return jnp.dot(a, b, preferred_element_type=F32)


def on_chip(x):
    return pltpu.with_memory_space_constraint(x, pltpu.VMEM)


def moved_down(values, period):
    row = lax.broadcasted_iota(jnp.int32, values.shape, 0)
    return jnp.where(lax.rem(row, period) == 0, 0.0, pltpu.roll(values, 1, 0))


def moved_up(values, period):
    row = lax.broadcasted_iota(jnp.int32, values.shape, 0)
    return jnp.where(
        lax.rem(row, period) == period - 1, 0.0, pltpu.roll(values, values.shape[0] - 1, 0)
    )


def in_hbm(x):
    return pltpu.with_memory_space_constraint(x, pltpu.HBM)


def conv_kernel(x_hbm, w_hbm, out_ref, planes, buf, weights, *rest, bands):
    *wide, sems, w_sem = rest
    count, height, width, channels = x_hbm.shape
    out_cols = width // 2
    band = height // bands
    out_rows = height // 2
    copies = []
    for frame in range(count):
        for b in range(bands):
            rows = pl.ds(b * band, band)
            copies.append(
                pltpu.make_async_copy(
                    x_hbm.at[frame, rows], buf.at[frame, rows], sems.at[frame * bands + b]
                )
            )
    copies[0].start()
    w_copy = pltpu.make_async_copy(w_hbm, weights, w_sem)
    w_copy.start()
    for copy in copies[1:]:
        copy.start()
    zero = jnp.zeros((out_cols, 2 * channels), BF16)
    chunk_pixels = out_ref.shape[2]
    owners = out_rows * out_cols // chunk_pixels

    def split(frame, b):
        copies[frame * bands + b].wait()
        for row in range(b * band, (b + 1) * band):
            slot = wide[row % len(wide)]
            slot[...] = buf[frame, row].astype(F32)
            even = slot[pl.ds(0, out_cols, stride=2), :]
            odd = slot[pl.ds(1, out_cols, stride=2), :]
            planes[frame, row + 1, :, :channels] = even.astype(BF16)
            planes[frame, row + 1, :, channels:] = odd.astype(BF16)

    def taps(lanes):
        return jnp.concatenate(
            [
                jnp.concatenate(
                    [planes[f, 2 * i + a, :, lanes] for f in range(count) for i in range(out_rows)], 0
                )
                for a in range(3)
            ],
            1,
        )

    for frame in range(count):
        planes[frame, 0] = zero
    for frame in range(count):
        for b in range(bands):
            split(frame, b)
    w_copy.wait()
    w_even = jnp.concatenate([weights[a, 1] for a in range(3)], 0)
    w_odd = jnp.concatenate(
        [jnp.concatenate([weights[a, 2], weights[a, 0]], 1) for a in range(3)], 0
    )
    odds = dot(taps(slice(channels, 2 * channels)), w_odd)
    total = dot(taps(slice(0, channels)), w_even) + odds[:, :channels]
    total = (total + moved_down(odds[:, channels:], out_cols)).astype(BF16)
    total = total.reshape(count, owners, chunk_pixels, channels)
    for frame in range(count):
        out_ref[:, frame] = total[frame]


def conv(frames, w_spatial, n):
    count, height, width, channels = frames.shape
    out_cols = width // 2
    bands = 2
    return pl.pallas_call(
        functools.partial(conv_kernel, bands=bands),
        in_specs=[HBM, HBM],
        out_specs=[VMEM, VMEM],
        out_shape=[
            pltpu.VMEM((n, count, height // 2 * out_cols // n, channels), BF16),
            pltpu.VMEM((count, height + 1, out_cols, 2 * channels), BF16),
        ],
        scratch_shapes=[
            pltpu.VMEM((count, height, width, channels), BF16),
            pltpu.VMEM(w_spatial.shape, BF16),
            *[pltpu.VMEM((width, channels), F32)] * 4,
            pltpu.SemaphoreType.DMA((count * bands,)),
            pltpu.SemaphoreType.DMA,
        ],
        compiler_params=pltpu.CompilerParams(vmem_limit_bytes=VMEM_LIMIT),
        name="conv",
    )(in_hbm(frames), in_hbm(w_spatial))


def row_shifts(dil_ref, off_ref, length, pixels):
    layers, taps = off_ref.shape
    return [
        [
            pl.multiple_of(
                jnp.minimum(off_ref[layer, tap] * dil_ref[layer], length) * pixels, pixels
            )
            for tap in range(taps)
        ]
        for layer in range(layers)
    ]


def moved_rows(ref, at, shifts, size, pixels):
    return jnp.concatenate(
        [ref[pl.ds(pl.multiple_of(at + s, pixels), size), :] for s in shifts], 1
    )


def temporal_kernel(
    length, dil_ref, off_ref, start_ref, cot_ref, w_ref, feat_hbm, back_hbm, mid_hbm, dz_hbm, *scratch
):
    layers, taps, channels = w_ref.shape[:3]
    state, dz = scratch[:layers], scratch[layers : 2 * layers]
    act, grad, feat, back, sems = scratch[2 * layers :]
    rows = start_ref.shape[0]
    pixels = rows // length
    size = min(1024, rows)
    starts = range(0, rows, size)
    shifts = row_shifts(dil_ref, off_ref, length, pixels)
    sent = []

    def send(source, target):
        sent.append(pltpu.make_async_copy(source, target, sems.at[len(sent)]))
        sent[-1].start()

    blank = jnp.zeros((rows, channels), BF16)
    for layer in range(layers):
        state[layer][pl.ds(0, rows), :] = blank
        dz[layer][pl.ds(rows, rows), :] = blank
    state[0][pl.ds(rows, rows), :] = start_ref[...]
    down = [w_ref[layer].reshape(taps * channels, channels) for layer in range(layers)]
    up = [
        jnp.concatenate([w_ref[layer, tap].T for tap in range(taps)], 0)
        for layer in range(layers)
    ]
    for layer in range(layers):
        last = layer == layers - 1
        for at in starts:
            here = pl.ds(at, size)
            moved = moved_rows(state[layer], rows + at, [-s for s in shifts[layer]], size, pixels)
            activ = jnp.tanh(dot(moved, down[layer]))
            held = state[layer][pl.ds(rows + at, size), :].astype(F32)
            following = (held + activ).astype(BF16)
            slope = 1.0 - activ * activ
            if last:
                feat[here, :] = following
                dz[layer][here, :] = (cot_ref[here, :].astype(F32) * slope).astype(BF16)
            else:
                state[layer + 1][pl.ds(rows + at, size), :] = following
                act[layer, here, :] = slope
        if last:
            send(feat, feat_hbm)
            send(dz[layer].at[pl.ds(0, rows)], dz_hbm.at[layer])
        else:
            send(state[layer + 1].at[pl.ds(rows, rows)], mid_hbm.at[layer])
    for layer in reversed(range(layers)):
        for at in starts:
            here = pl.ds(at, size)
            if layer == layers - 1:
                before = cot_ref[here, :].astype(F32)
            else:
                before = grad[here, :]
            after = before + dot(moved_rows(dz[layer], at, shifts[layer], size, pixels), up[layer])
            if layer > 0:
                grad[here, :] = after
                dz[layer - 1][here, :] = (after * act[layer - 1, here, :]).astype(BF16)
            else:
                back[here, :] = after.astype(BF16)
                send(back.at[here], back_hbm.at[here])
        if layer > 0:
            send(dz[layer - 1].at[pl.ds(0, rows)], dz_hbm.at[layer - 1])
    for copy in sent:
        copy.wait()


def temporal(start, cotangent, w_temporal, dilations, offsets, length):
    rows, channels = start.shape
    layers = w_temporal.shape[0]
    pieces = rows // min(1024, rows)
    return pl.pallas_call(
        functools.partial(temporal_kernel, length),
        in_specs=[SMEM, SMEM, VMEM, VMEM, VMEM],
        out_specs=[HBM] * 4,
        out_shape=[
            pltpu.HBM((rows, channels), BF16),
            pltpu.HBM((rows, channels), BF16),
            pltpu.HBM((max(layers - 1, 1), rows, channels), BF16),
            pltpu.HBM((layers, rows, channels), BF16),
        ],
        scratch_shapes=[pltpu.VMEM((2 * rows, channels), BF16)] * (2 * layers)
        + [
            pltpu.VMEM((max(layers - 1, 1), rows, channels), F32),
            pltpu.VMEM((rows, channels), F32),
            pltpu.VMEM((rows, channels), BF16),
            pltpu.VMEM((rows, channels), BF16),
            pltpu.SemaphoreType.DMA((2 * layers + pieces,)),
        ],
        compiler_params=pltpu.CompilerParams(vmem_limit_bytes=VMEM_LIMIT),
        name="temporal",
    )(dilations, offsets, on_chip(start), on_chip(cotangent), on_chip(w_temporal))


def deal(core_ref, whole, own_ref, other_ref):
    half = own_ref.shape[0]
    core = core_ref[0]
    own_ref[...] = whole[pl.ds(pl.multiple_of(core * half, half), half), :]
    other_ref[...] = whole[pl.ds(pl.multiple_of((1 - core) * half, half), half), :].astype(BF16)


def temporal_outer_kernel(
    length, core_ref, dil_ref, off_ref, start_ref, mid_hbm, dz_hbm, own_ref, other_ref, state, dz, whole, sems
):
    layers, taps = off_ref.shape
    rows, channels = start_ref.shape
    pixels = rows // length
    size = min(1024, rows)
    copies = []
    for layer in range(layers):
        copies.append([pltpu.make_async_copy(dz_hbm.at[layer], dz.at[layer], sems.at[2 * layer])])
        if layer > 0:
            target = state.at[layer, pl.ds(rows, rows)]
            copies[-1].append(
                pltpu.make_async_copy(mid_hbm.at[layer - 1], target, sems.at[2 * layer + 1])
            )
        for copy in copies[-1]:
            copy.start()
    shifts = row_shifts(dil_ref, off_ref, length, pixels)
    blank = jnp.zeros((rows, channels), BF16)
    for layer in range(layers):
        state[layer, pl.ds(0, rows), :] = blank
        if layer == 0:
            state[layer, pl.ds(rows, rows), :] = start_ref[...]
        for copy in copies[layer]:
            copy.wait()
        total = jnp.zeros((channels, taps * channels), F32)
        for at in range(0, rows, size):
            moved = moved_rows(state.at[layer], rows + at, [-s for s in shifts[layer]], size, pixels)
            values = dz[layer, pl.ds(at, size), :]
            total += lax.dot_general(values, moved, ROWS, preferred_element_type=F32)
        for tap in range(taps):
            place = pl.ds((layer * taps + tap) * channels, channels)
            whole[place, :] = total[:, tap * channels : (tap + 1) * channels].T
    deal(core_ref, whole, own_ref, other_ref)


def temporal_outer(start, mid, dz, dilations, offsets, length, core):
    rows, channels = start.shape
    layers, taps = offsets.shape
    half = layers * taps * channels // 2
    return pl.pallas_call(
        functools.partial(temporal_outer_kernel, length),
        in_specs=[SMEM, SMEM, SMEM, VMEM, HBM, HBM],
        out_specs=[VMEM, VMEM],
        out_shape=[pltpu.VMEM((half, channels), F32), pltpu.VMEM((half, channels), BF16)],
        scratch_shapes=[
            pltpu.VMEM((layers, 2 * rows, channels), BF16),
            pltpu.VMEM((layers, rows, channels), BF16),
            pltpu.VMEM((2 * half, channels), F32),
            pltpu.SemaphoreType.DMA((2 * layers,)),
        ],
        compiler_params=pltpu.CompilerParams(vmem_limit_bytes=VMEM_LIMIT),
        name="temporal_outer",
    )(core, dilations, offsets, on_chip(start), in_hbm(mid), in_hbm(dz))


def spatial_outer_kernel(core_ref, planes, back_ref, own_ref, other_ref, whole):
    count, height, out_cols, channels = planes.shape
    channels //= 2
    out_rows = (height - 1) // 2
    totals = [jnp.zeros((2 * channels, 2 * channels), F32) for _ in range(3)]
    for frame in range(count):
        back = back_ref[:, frame].reshape(out_rows * out_cols, channels)
        up = moved_up(back.astype(F32), out_cols).astype(BF16)
        both = jnp.concatenate([back, up], 1).T
        for a in range(3):
            moved = jnp.concatenate([planes[frame, 2 * i + a] for i in range(out_rows)], 0)
            totals[a] += dot(both, moved)
    for a in range(3):
        products = (
            totals[a][channels:, channels:],
            totals[a][:channels, :channels],
            totals[a][:channels, channels:],
        )
        for b, product in enumerate(products):
            whole[pl.ds((3 * a + b) * channels, channels), :] = product.T
    deal(core_ref, whole, own_ref, other_ref)


def spatial_outer(planes, back, core):
    channels = planes.shape[-1] // 2
    half = 9 * channels // 2
    return pl.pallas_call(
        spatial_outer_kernel,
        in_specs=[SMEM, VMEM, VMEM],
        out_specs=[VMEM, VMEM],
        out_shape=[pltpu.VMEM((half, channels), F32), pltpu.VMEM((half, channels), BF16)],
        scratch_shapes=[pltpu.VMEM((2 * half, channels), F32)],
        compiler_params=pltpu.CompilerParams(vmem_limit_bytes=VMEM_LIMIT),
        name="spatial_outer",
    )(core, on_chip(planes), on_chip(back))


def swap(x, n, mask):
    return lax.ppermute(x, "seq", [(i, i ^ mask) for i in range(n)])


def sum_parts(values, n, low, count):
    me = lax.rem(lax.axis_index("seq") >> low, 1 << count)
    parts = values.reshape(1 << count, values.shape[0] >> count, -1)
    total = lax.dynamic_index_in_dim(parts, me, 0, keepdims=False)
    for peer in range(1, 1 << count):
        theirs = lax.dynamic_index_in_dim(parts, me ^ peer, 0, keepdims=False)
        total = total + swap(theirs.astype(BF16), n, peer << low).astype(F32)
    return total


def sum_whole(values, n, bits):
    for bit in bits:
        sent = values.astype(BF16)
        values = sent.astype(F32) + swap(sent, n, 1 << bit).astype(F32)
    return values


def gather_parts(values, n, low, count):
    me = lax.axis_index("seq") >> low
    held = [values] + [swap(values, n, peer << low) for peer in range(1, 1 << count)]
    for bit in range(count):
        upper = (me >> bit) & 1
        step = 1 << bit
        held = [jnp.where(upper == 0, held[q], held[q ^ step]) for q in range(1 << count)]
    return jnp.concatenate(held, 0)


def widen_kernel(core_ref, own_ref, got_ref, spatial_ref, temporal_ref):
    cut = spatial_ref.shape[2]
    core = core_ref[0]
    for place, ref in ((core, own_ref), (1 - core, got_ref)):
        spatial_ref[place] = ref[:, :cut].astype(F32)
        temporal_ref[place] = ref[:, cut:].astype(F32)


def widen(own, n, core, spatial_rows, temporal_rows):
    own = own.reshape(-1, spatial_rows + temporal_rows, own.shape[-1])
    parts, channels = own.shape[0], own.shape[-1]
    return pl.pallas_call(
        widen_kernel,
        in_specs=[SMEM, VMEM, VMEM],
        out_specs=[VMEM, VMEM],
        out_shape=[
            jax.ShapeDtypeStruct((2, parts, spatial_rows, channels), F32),
            jax.ShapeDtypeStruct((2, parts, temporal_rows, channels), F32),
        ],
        compiler_params=pltpu.CompilerParams(vmem_limit_bytes=VMEM_LIMIT),
        name="widen",
    )(core, on_chip(own), on_chip(swap(own, n, 1)))


def exchange(x):
    return lax.all_to_all(x, "seq", split_axis=0, concat_axis=0, tiled=True)


def local(n, frames, w_spatial, w_temporal, dilations, offsets, cotangent):
    count, height, width, channels = frames.shape
    length, pixels = cotangent.shape[:2]
    bits = n.bit_length() - 1
    maps, planes = conv(frames, w_spatial, n)
    start = exchange(maps.reshape(n, count * pixels, channels)).reshape(length * pixels, channels)
    features, grad_maps, mid, dz = temporal(
        start, cotangent.reshape(length * pixels, channels), w_temporal, dilations, offsets, length
    )
    back = exchange(grad_maps.reshape(n, count * pixels, channels))
    core = lax.rem(lax.axis_index("seq"), 2).astype(jnp.int32).reshape(1)
    size = min(2, bits - 1)
    one = min(1, bits - 1)

    def add_cores(own, other):
        return own + swap(other, n, 1).astype(F32)

    of_temporal = sum_parts(add_cores(*temporal_outer(start, mid, dz, dilations, offsets, length, core)), n, 1, one)
    of_temporal = sum_whole(of_temporal, n, range(1 + one, min(2 + one, bits)))
    own, other = spatial_outer(planes, back.reshape(n, count, pixels, channels), core)
    of_spatial = add_cores(own, other)
    of_spatial, of_temporal = lax.optimization_barrier((of_spatial, of_temporal))
    of_spatial = sum_parts(of_spatial, n, 1, size)
    of_temporal = sum_whole(of_temporal, n, range(min(2 + one, bits), bits)).astype(BF16)
    of_temporal = gather_parts(gather_parts(of_temporal, n, 1, one), n, 0, 1)
    of_temporal = of_temporal.astype(F32).reshape(w_temporal.shape)
    of_spatial = sum_whole(of_spatial, n, range(1 + size, bits)).astype(BF16)
    of_spatial = gather_parts(gather_parts(of_spatial, n, 1, size), n, 0, 1)
    of_spatial = of_spatial.astype(F32).reshape(w_spatial.shape)
    return (
        features.reshape(length, pixels, channels),
        of_spatial.reshape(w_spatial.shape),
        of_temporal.reshape(w_temporal.shape),
    )


def solution(mesh):
    in_specs = (
        P(("groups", "seq"), None, None, None),
        P(),
        P(),
        P(),
        P(),
        P("groups", "seq", None),
    )
    out_specs = (
        P("groups", "seq", None),
        P("groups", None, None, None),
        P("groups", None, None, None),
    )
    return jax.shard_map(
        functools.partial(local, mesh.shape["seq"]),
        mesh=mesh,
        in_specs=in_specs,
        out_specs=out_specs,
        check_vma=False,
    )
```

```python
import functools

import jax
import jax.numpy as jnp
from jax import lax
from jax.experimental import pallas as pl
from jax.experimental.pallas import tpu as pltpu
from jax.sharding import PartitionSpec as P

F32, BF16 = jnp.float32, jnp.bfloat16
VMEM_LIMIT = 24 * 1024 * 1024
ROWS = (((0,), (0,)), ((), ()))
VMEM = pl.BlockSpec(memory_space=pltpu.VMEM)
HBM = pl.BlockSpec(memory_space=pltpu.HBM)
SMEM = pl.BlockSpec(memory_space=pltpu.SMEM)


def dot(a, b):
    return jnp.dot(a, b, preferred_element_type=F32)


def on_chip(x):
    return pltpu.with_memory_space_constraint(x, pltpu.VMEM)


def moved_down(values, period):
    row = lax.broadcasted_iota(jnp.int32, values.shape, 0)
    return jnp.where(lax.rem(row, period) == 0, 0.0, pltpu.roll(values, 1, 0))


def moved_up(values, period):
    row = lax.broadcasted_iota(jnp.int32, values.shape, 0)
    return jnp.where(
        lax.rem(row, period) == period - 1, 0.0, pltpu.roll(values, values.shape[0] - 1, 0)
    )


def in_hbm(x):
    return pltpu.with_memory_space_constraint(x, pltpu.HBM)


def conv_kernel(x_hbm, w_hbm, out_ref, planes, buf, weights, *rest, bands):
    *wide, sems, w_sem = rest
    count, height, width, channels = x_hbm.shape
    out_cols = width // 2
    band = height // bands
    out_rows = height // 2
    copies = []
    for frame in range(count):
        for b in range(bands):
            rows = pl.ds(b * band, band)
            copies.append(
                pltpu.make_async_copy(
                    x_hbm.at[frame, rows], buf.at[frame, rows], sems.at[frame * bands + b]
                )
            )
    copies[0].start()
    w_copy = pltpu.make_async_copy(w_hbm, weights, w_sem)
    w_copy.start()
    for copy in copies[1:]:
        copy.start()
    zero = jnp.zeros((out_cols, 2 * channels), BF16)
    chunk_pixels = out_ref.shape[2]
    owners = out_rows * out_cols // chunk_pixels

    def split(frame, b):
        copies[frame * bands + b].wait()
        for row in range(b * band, (b + 1) * band):
            slot = wide[row % len(wide)]
            slot[...] = buf[frame, row].astype(F32)
            even = slot[pl.ds(0, out_cols, stride=2), :]
            odd = slot[pl.ds(1, out_cols, stride=2), :]
            planes[frame, row + 1, :, :channels] = even.astype(BF16)
            planes[frame, row + 1, :, channels:] = odd.astype(BF16)

    def taps(lanes):
        return jnp.concatenate(
            [
                jnp.concatenate(
                    [planes[f, 2 * i + a, :, lanes] for f in range(count) for i in range(out_rows)], 0
                )
                for a in range(3)
            ],
            1,
        )

    for frame in range(count):
        planes[frame, 0] = zero
    for frame in range(count):
        for b in range(bands):
            split(frame, b)
    w_copy.wait()
    w_even = jnp.concatenate([weights[a, 1] for a in range(3)], 0)
    w_odd = jnp.concatenate(
        [jnp.concatenate([weights[a, 2], weights[a, 0]], 1) for a in range(3)], 0
    )
    odds = dot(taps(slice(channels, 2 * channels)), w_odd)
    total = dot(taps(slice(0, channels)), w_even) + odds[:, :channels]
    total = (total + moved_down(odds[:, channels:], out_cols)).astype(BF16)
    total = total.reshape(count, owners, chunk_pixels, channels)
    for frame in range(count):
        out_ref[:, frame] = total[frame]


def conv(frames, w_spatial, n):
    count, height, width, channels = frames.shape
    out_cols = width // 2
    bands = 2
    return pl.pallas_call(
        functools.partial(conv_kernel, bands=bands),
        in_specs=[HBM, HBM],
        out_specs=[VMEM, VMEM],
        out_shape=[
            pltpu.VMEM((n, count, height // 2 * out_cols // n, channels), BF16),
            pltpu.VMEM((count, height + 1, out_cols, 2 * channels), BF16),
        ],
        scratch_shapes=[
            pltpu.VMEM((count, height, width, channels), BF16),
            pltpu.VMEM(w_spatial.shape, BF16),
            *[pltpu.VMEM((width, channels), F32)] * 4,
            pltpu.SemaphoreType.DMA((count * bands,)),
            pltpu.SemaphoreType.DMA,
        ],
        compiler_params=pltpu.CompilerParams(vmem_limit_bytes=VMEM_LIMIT),
        name="conv",
    )(in_hbm(frames), in_hbm(w_spatial))


def row_shifts(dil_ref, off_ref, length, pixels):
    layers, taps = off_ref.shape
    return [
        [
            pl.multiple_of(
                jnp.minimum(off_ref[layer, tap] * dil_ref[layer], length) * pixels, pixels
            )
            for tap in range(taps)
        ]
        for layer in range(layers)
    ]


def moved_rows(ref, at, shifts, size, pixels):
    return jnp.concatenate(
        [ref[pl.ds(pl.multiple_of(at + s, pixels), size), :] for s in shifts], 1
    )


def temporal_kernel(
    length, dil_ref, off_ref, start_ref, cot_ref, w_ref, feat_hbm, back_hbm, mid_hbm, dz_hbm, *scratch
):
    layers, taps, channels = w_ref.shape[:3]
    rows = start_ref.shape[0]
    held_in = scratch[:layers]
    act, grad, feat, back, sems = scratch[layers:]
    state = [ref.at[pl.ds(rows, 2 * rows)] for ref in held_in]
    dz = [ref.at[pl.ds(0, 2 * rows)] for ref in reversed(held_in)]
    pixels = rows // length
    size = min(1024, rows)
    starts = range(0, rows, size)
    shifts = row_shifts(dil_ref, off_ref, length, pixels)
    sent = []

    def send(source, target):
        sent.append(pltpu.make_async_copy(source, target, sems.at[len(sent)]))
        sent[-1].start()

    blank = jnp.zeros((rows, channels), BF16)
    for layer in range(layers):
        held_in[layer][pl.ds(rows, rows), :] = blank
    state[0][pl.ds(rows, rows), :] = start_ref[...]
    down = [w_ref[layer].reshape(taps * channels, channels) for layer in range(layers)]
    up = [
        jnp.concatenate([w_ref[layer, tap].T for tap in range(taps)], 0)
        for layer in range(layers)
    ]
    for layer in range(layers):
        last = layer == layers - 1
        for at in starts:
            here = pl.ds(at, size)
            moved = moved_rows(state[layer], rows + at, [-s for s in shifts[layer]], size, pixels)
            activ = jnp.tanh(dot(moved, down[layer]))
            held = state[layer][pl.ds(rows + at, size), :].astype(F32)
            following = (held + activ).astype(BF16)
            slope = 1.0 - activ * activ
            if last:
                feat[here, :] = following
                dz[layer][here, :] = (cot_ref[here, :].astype(F32) * slope).astype(BF16)
            else:
                state[layer + 1][pl.ds(rows + at, size), :] = following
                act[layer, here, :] = slope
        if last:
            send(feat, feat_hbm)
            send(dz[layer].at[pl.ds(0, rows)], dz_hbm.at[layer])
        else:
            send(state[layer + 1].at[pl.ds(rows, rows)], mid_hbm.at[layer])
    for layer in reversed(range(layers)):
        for at in starts:
            here = pl.ds(at, size)
            if layer == layers - 1:
                before = cot_ref[here, :].astype(F32)
            else:
                before = grad[here, :]
            after = before + dot(moved_rows(dz[layer], at, shifts[layer], size, pixels), up[layer])
            if layer > 0:
                grad[here, :] = after
                dz[layer - 1][here, :] = (after * act[layer - 1, here, :]).astype(BF16)
            else:
                back[here, :] = after.astype(BF16)
                send(back.at[here], back_hbm.at[here])
        if layer > 0:
            send(dz[layer - 1].at[pl.ds(0, rows)], dz_hbm.at[layer - 1])
    for copy in sent:
        copy.wait()


def temporal(start, cotangent, w_temporal, dilations, offsets, length):
    rows, channels = start.shape
    layers = w_temporal.shape[0]
    pieces = rows // min(1024, rows)
    return pl.pallas_call(
        functools.partial(temporal_kernel, length),
        in_specs=[SMEM, SMEM, VMEM, VMEM, VMEM],
        out_specs=[HBM] * 4,
        out_shape=[
            pltpu.HBM((rows, channels), BF16),
            pltpu.HBM((rows, channels), BF16),
            pltpu.HBM((max(layers - 1, 1), rows, channels), BF16),
            pltpu.HBM((layers, rows, channels), BF16),
        ],
        scratch_shapes=[pltpu.VMEM((3 * rows, channels), BF16)] * layers
        + [
            pltpu.VMEM((max(layers - 1, 1), rows, channels), F32),
            pltpu.VMEM((rows, channels), F32),
            pltpu.VMEM((rows, channels), BF16),
            pltpu.VMEM((rows, channels), BF16),
            pltpu.SemaphoreType.DMA((2 * layers + pieces,)),
        ],
        compiler_params=pltpu.CompilerParams(vmem_limit_bytes=VMEM_LIMIT),
        name="temporal",
    )(dilations, offsets, on_chip(start), on_chip(cotangent), on_chip(w_temporal))


def deal(core_ref, whole, own_ref, other_ref):
    half = own_ref.shape[0]
    core = core_ref[0]
    own_ref[...] = whole[pl.ds(pl.multiple_of(core * half, half), half), :]
    other_ref[...] = whole[pl.ds(pl.multiple_of((1 - core) * half, half), half), :].astype(BF16)


def temporal_outer_kernel(
    length, core_ref, dil_ref, off_ref, start_ref, mid_hbm, dz_hbm, own_ref, other_ref, state, dz, whole, sems
):
    layers, taps = off_ref.shape
    rows, channels = start_ref.shape
    pixels = rows // length
    size = min(1024, rows)
    copies = []
    for layer in range(layers):
        copies.append([pltpu.make_async_copy(dz_hbm.at[layer], dz.at[layer], sems.at[2 * layer])])
        if layer > 0:
            target = state.at[layer, pl.ds(rows, rows)]
            copies[-1].append(
                pltpu.make_async_copy(mid_hbm.at[layer - 1], target, sems.at[2 * layer + 1])
            )
        for copy in copies[-1]:
            copy.start()
    shifts = row_shifts(dil_ref, off_ref, length, pixels)
    blank = jnp.zeros((rows, channels), BF16)
    for layer in range(layers):
        state[layer, pl.ds(0, rows), :] = blank
        if layer == 0:
            state[layer, pl.ds(rows, rows), :] = start_ref[...]
        for copy in copies[layer]:
            copy.wait()
        total = jnp.zeros((channels, taps * channels), F32)
        for at in range(0, rows, size):
            moved = moved_rows(state.at[layer], rows + at, [-s for s in shifts[layer]], size, pixels)
            values = dz[layer, pl.ds(at, size), :]
            total += lax.dot_general(values, moved, ROWS, preferred_element_type=F32)
        for tap in range(taps):
            place = pl.ds((layer * taps + tap) * channels, channels)
            whole[place, :] = total[:, tap * channels : (tap + 1) * channels].T
    deal(core_ref, whole, own_ref, other_ref)


def temporal_outer(start, mid, dz, dilations, offsets, length, core):
    rows, channels = start.shape
    layers, taps = offsets.shape
    half = layers * taps * channels // 2
    return pl.pallas_call(
        functools.partial(temporal_outer_kernel, length),
        in_specs=[SMEM, SMEM, SMEM, VMEM, HBM, HBM],
        out_specs=[VMEM, VMEM],
        out_shape=[pltpu.VMEM((half, channels), F32), pltpu.VMEM((half, channels), BF16)],
        scratch_shapes=[
            pltpu.VMEM((layers, 2 * rows, channels), BF16),
            pltpu.VMEM((layers, rows, channels), BF16),
            pltpu.VMEM((2 * half, channels), F32),
            pltpu.SemaphoreType.DMA((2 * layers,)),
        ],
        compiler_params=pltpu.CompilerParams(vmem_limit_bytes=VMEM_LIMIT),
        name="temporal_outer",
    )(core, dilations, offsets, on_chip(start), in_hbm(mid), in_hbm(dz))


def spatial_outer_kernel(core_ref, planes, back_ref, own_ref, other_ref, whole):
    count, height, out_cols, channels = planes.shape
    channels //= 2
    out_rows = (height - 1) // 2
    totals = [jnp.zeros((2 * channels, 2 * channels), F32) for _ in range(3)]
    for frame in range(count):
        back = back_ref[:, frame].reshape(out_rows * out_cols, channels)
        up = moved_up(back.astype(F32), out_cols).astype(BF16)
        both = jnp.concatenate([back, up], 1).T
        for a in range(3):
            moved = jnp.concatenate([planes[frame, 2 * i + a] for i in range(out_rows)], 0)
            totals[a] += dot(both, moved)
    for a in range(3):
        products = (
            totals[a][channels:, channels:],
            totals[a][:channels, :channels],
            totals[a][:channels, channels:],
        )
        for b, product in enumerate(products):
            whole[pl.ds((3 * a + b) * channels, channels), :] = product.T
    deal(core_ref, whole, own_ref, other_ref)


def spatial_outer(planes, back, core):
    channels = planes.shape[-1] // 2
    half = 9 * channels // 2
    return pl.pallas_call(
        spatial_outer_kernel,
        in_specs=[SMEM, VMEM, VMEM],
        out_specs=[VMEM, VMEM],
        out_shape=[pltpu.VMEM((half, channels), F32), pltpu.VMEM((half, channels), BF16)],
        scratch_shapes=[pltpu.VMEM((2 * half, channels), F32)],
        compiler_params=pltpu.CompilerParams(vmem_limit_bytes=VMEM_LIMIT),
        name="spatial_outer",
    )(core, on_chip(planes), on_chip(back))


def swap(x, n, mask):
    return lax.ppermute(x, "seq", [(i, i ^ mask) for i in range(n)])


def sum_parts(values, n, low, count):
    me = lax.rem(lax.axis_index("seq") >> low, 1 << count)
    parts = values.reshape(1 << count, values.shape[0] >> count, -1)
    total = lax.dynamic_index_in_dim(parts, me, 0, keepdims=False)
    for peer in reversed(range(1, 1 << count)):
        theirs = lax.dynamic_index_in_dim(parts, me ^ peer, 0, keepdims=False)
        total = total + swap(theirs.astype(BF16), n, peer << low).astype(F32)
    return total


def sum_whole(values, n, bits):
    for bit in bits:
        sent = values.astype(BF16)
        values = sent.astype(F32) + swap(sent, n, 1 << bit).astype(F32)
    return values


def gather_parts(values, n, low, count):
    me = lax.axis_index("seq") >> low
    held = [values] + [swap(values, n, peer << low) for peer in range(1, 1 << count)]
    for bit in range(count):
        upper = (me >> bit) & 1
        step = 1 << bit
        held = [jnp.where(upper == 0, held[q], held[q ^ step]) for q in range(1 << count)]
    return jnp.concatenate(held, 0)


def widen_kernel(core_ref, own_ref, got_ref, spatial_ref, temporal_ref):
    cut = spatial_ref.shape[2]
    core = core_ref[0]
    for place, ref in ((core, own_ref), (1 - core, got_ref)):
        spatial_ref[place] = ref[:, :cut].astype(F32)
        temporal_ref[place] = ref[:, cut:].astype(F32)


def widen(own, n, core, spatial_rows, temporal_rows):
    own = own.reshape(-1, spatial_rows + temporal_rows, own.shape[-1])
    parts, channels = own.shape[0], own.shape[-1]
    return pl.pallas_call(
        widen_kernel,
        in_specs=[SMEM, VMEM, VMEM],
        out_specs=[VMEM, VMEM],
        out_shape=[
            jax.ShapeDtypeStruct((2, parts, spatial_rows, channels), F32),
            jax.ShapeDtypeStruct((2, parts, temporal_rows, channels), F32),
        ],
        compiler_params=pltpu.CompilerParams(vmem_limit_bytes=VMEM_LIMIT),
        name="widen",
    )(core, on_chip(own), on_chip(swap(own, n, 1)))


def exchange(x):
    return lax.all_to_all(x, "seq", split_axis=0, concat_axis=0, tiled=True)


def local(n, frames, w_spatial, w_temporal, dilations, offsets, cotangent):
    count, height, width, channels = frames.shape
    length, pixels = cotangent.shape[:2]
    bits = n.bit_length() - 1
    maps, planes = conv(frames, w_spatial, n)
    start = exchange(maps.reshape(n, count * pixels, channels)).reshape(length * pixels, channels)
    features, grad_maps, mid, dz = temporal(
        start, cotangent.reshape(length * pixels, channels), w_temporal, dilations, offsets, length
    )
    back = exchange(grad_maps.reshape(n, count * pixels, channels))
    core = lax.rem(lax.axis_index("seq"), 2).astype(jnp.int32).reshape(1)
    size = min(2, bits - 1)
    one = min(1, bits - 1)

    def add_cores(own, other):
        return own + swap(other, n, 1).astype(F32)

    of_temporal = sum_parts(add_cores(*temporal_outer(start, mid, dz, dilations, offsets, length, core)), n, 1, one)
    of_temporal = sum_whole(of_temporal, n, range(1 + one, min(2 + one, bits)))
    own, other = spatial_outer(planes, back.reshape(n, count, pixels, channels), core)
    of_spatial = add_cores(own, other)
    of_spatial, of_temporal = lax.optimization_barrier((of_spatial, of_temporal))
    of_spatial = sum_parts(of_spatial, n, 1, size)
    of_temporal = sum_whole(of_temporal, n, range(min(2 + one, bits), bits)).astype(BF16)
    of_temporal = gather_parts(gather_parts(of_temporal, n, 1, one), n, 0, 1)
    of_temporal = of_temporal.astype(F32).reshape(w_temporal.shape)
    of_spatial = sum_whole(of_spatial, n, range(1 + size, bits)).astype(BF16)
    of_spatial = gather_parts(gather_parts(of_spatial, n, 1, size), n, 0, 1)
    of_spatial = of_spatial.astype(F32).reshape(w_spatial.shape)
    return (
        features.reshape(length, pixels, channels),
        of_spatial.reshape(w_spatial.shape),
        of_temporal.reshape(w_temporal.shape),
    )


def solution(mesh):
    in_specs = (
        P(("groups", "seq"), None, None, None),
        P(),
        P(),
        P(),
        P(),
        P("groups", "seq", None),
    )
    out_specs = (
        P("groups", "seq", None),
        P("groups", None, None, None),
        P("groups", None, None, None),
    )
    return jax.shard_map(
        functools.partial(local, mesh.shape["seq"]),
        mesh=mesh,
        in_specs=in_specs,
        out_specs=out_specs,
        check_vma=False,
    )
```
